32 devices in a mesh: seq: 8 (over z, x), tp: 4 (over y, core).
Axes of the slice: x: 2, y: 2, z: 4, core: 2. Of those that a mesh axis runs over, the one named last changes fastest.
Arguments:
- draft_q: bfloat16 [256, 4096], P('seq', 'tp'), may hold values from -16 to 16
- draft_kv: bfloat16 [2, 256, 4096], P(None, 'seq', 'tp'), may hold values from -6 to 6
- kv_pool: bfloat16 [2, 128, 128, 4096], P(None, 'seq', None, 'tp'), may hold values from -8 to 8
- page_table: int32 [4, 32], replicated, may hold values from -1 to 127, as said below
- cache_len: int32 [4], replicated, may hold values from 2048 to 4096, as said below
- tree_mask: int32 [4, 64, 64], replicated, may hold values from 0 to 1, as said below
- accepted_rows: int32 [4, 64], replicated, may hold values from -1 to 63, as said below
- out_weight: bfloat16 [4096, 4096], P('tp'), may hold values from -0.125 to 0.125
Outputs:
- layer_out: bfloat16 [256, 4096], P('seq', 'tp')
- accepted_kv: bfloat16 [2, 4, 128, 4096], P(None, None, None, 'tp')
The draws below stay inside these ranges and needn't reach their ends.
Inputs may be any that keep to these rules, and one draw needn't show every extreme that they name: `page_table`: entries past a request's cached pages are -1; the slots in use are distinct over all requests. `cache_len`: some request holds exactly 4096 cached tokens. `tree_mask`: entry (r, i, k) is 1 where draft row k is row i itself or one of its ancestors in request r's token tree; a parent precedes its children, row 0 is the root. `accepted_rows`: each row lists in ascending order the draft rows of one root-to-node path of the tree, then -1.
All inputs are finite; a program needn't handle non-finite values.
Results may differ from the reference program's by a relative error of at most 0.0051.
Values may be sent and summed in bfloat16 or wider, within the bound.
A program may use at most 128 MiB of HBM per device.

```python
import math
import jax
import jax.numpy as jnp
from jax import lax

D = 4096
HEADS = 32
HD = 128
PAGE = 128
CACHE_MAX = 4096
DRAFT = 64
REQ = 4
WIDTH = 4096
MAXP = 32
ROWS = 256
POOL = 128


def draw_layout(key):
    base_key = jax.random.fold_in(key, 11)
    key_len, key_long, key_perm = jax.random.split(base_key, 3)
    lengths = jax.random.randint(key_len, (REQ,), CACHE_MAX // 2, CACHE_MAX + 1)
    longest = jax.random.randint(key_long, (), 0, REQ)
    lengths = jnp.where(jnp.arange(REQ) == longest, CACHE_MAX, lengths).astype(jnp.int32)
    layout = jax.random.permutation(key_perm, POOL)[:REQ * MAXP].reshape(REQ, MAXP).astype(jnp.int32)
    first_slot = layout[longest, 0]
    top_slot = jnp.int32(POOL - 1)
    layout = jnp.where(layout == first_slot, top_slot, jnp.where(layout == top_slot, first_slot, layout))
    in_use = jnp.arange(MAXP)[None, :] * PAGE < lengths[:, None]
    layout = jnp.where(in_use, layout, -1).astype(jnp.int32)
    return (lengths, layout)


def draw_tree(key):
    base_key = jax.random.fold_in(key, 59)
    key_parent, key_node = jax.random.split(base_key)
    columns = jnp.arange(DRAFT)
    parent = jax.random.randint(key_parent, (REQ, DRAFT), 0, jnp.maximum(columns, 1)[None, :])
    identity = jnp.eye(DRAFT, dtype=jnp.int32)
    ancestry = jnp.broadcast_to(identity, (REQ, DRAFT, DRAFT))

    def grow(column, ancestry):
        above = ancestry[jnp.arange(REQ), parent[:, column]]
        fresh = jnp.maximum(above, identity[column][None, :])
        return ancestry.at[:, column].set(fresh)
    ancestry = lax.fori_loop(1, DRAFT, grow, ancestry)
    chosen = jax.random.randint(key_node, (REQ,), 0, DRAFT)
    chosen = jnp.where(jnp.arange(REQ) == 0, DRAFT - 1, chosen)
    on_chain = ancestry[jnp.arange(REQ), chosen]
    chain_rank = jnp.cumsum(on_chain, axis=1) - 1
    matches = (on_chain[:, None, :] == 1) & (chain_rank[:, None, :] == columns[None, :, None])
    chain_rows = jnp.sum(jnp.where(matches, columns[None, None, :], 0), axis=2)
    chain_count = jnp.sum(on_chain, axis=1)
    chain_rows = jnp.where(columns[None, :] < chain_count[:, None], chain_rows, -1)
    return (ancestry.astype(jnp.int32), chain_rows.astype(jnp.int32))


def draw_page_table(key, part):
    lengths, layout = draw_layout(key)
    return layout


def draw_cache_len(key, part):
    lengths, layout = draw_layout(key)
    return lengths


def draw_tree_mask(key, part):
    ancestry, chain_rows = draw_tree(key)
    return ancestry


def draw_accepted_rows(key, part):
    ancestry, chain_rows = draw_tree(key)
    return chain_rows


def draw_draft_q(key, part):
    key_main = jax.random.fold_in(jax.random.fold_in(key, 31), 0)
    queries = jax.random.normal(key_main, (ROWS, WIDTH))
    return jnp.clip(queries, -16.0, 16.0).astype(jnp.bfloat16)


def draw_kv_pool(key, part):
    key_main, key_scale = jax.random.split(jax.random.fold_in(key, 23))
    entries = jax.random.normal(key_main, (2, POOL, PAGE, WIDTH))
    key_scales = jnp.exp(jax.random.uniform(key_scale, (1, POOL, PAGE, 1), minval=math.log(0.3), maxval=math.log(3.0)))
    scales = jnp.concatenate([key_scales, jnp.ones_like(key_scales)], axis=0)
    entries = jnp.clip(entries * scales, -8.0, 8.0)
    return entries.astype(jnp.bfloat16)


def spiked(drawn, own_key, source, target, shards_of, factor):
    def block_of(dim):
        return (jnp.arange(drawn.shape[dim]) // (drawn.shape[dim] // shards_of)).reshape((-1,) + (1,) * (drawn.ndim - 1 - dim))

    near = jax.random.permutation(own_key, shards_of)[block_of(target)]
    other_side = (block_of(target) + shards_of // 2) % shards_of
    return jnp.where((block_of(source) == near) | (block_of(source) == other_side), factor * drawn, drawn)


def steps_of(own_key, dims, cuts, low, top_value):
    def one(dim, blocks):
        heights = jax.random.uniform(jax.random.fold_in(jax.random.fold_in(own_key, 6), dim), (blocks,), jnp.float32, low / len(cuts), top_value / len(cuts))
        return jnp.repeat(jnp.exp(heights), dims[dim] // blocks).reshape((-1,) + (1,) * (len(dims) - dim - 1))

    level = one(*cuts[0])
    for cut in cuts[1:]:
        level = level * one(*cut)
    return level


def bell_draw(stream_key, extent, width, limit, cuts=(), held_as=jnp.bfloat16):
    loudness = steps_of(stream_key, extent, cuts, -0.22, 0.18) if cuts else 1.0
    values = jax.random.normal(stream_key, extent, jnp.float32) * width * loudness
    return jnp.minimum(jnp.maximum(values, -limit), limit).astype(held_as)


def heavy_noise(stream_key, extent, scale, most, pieces, heavy, kind=jnp.bfloat16):
    drawn = scale * jax.random.normal(stream_key, extent, jnp.float32)
    if pieces:
        drawn = drawn * steps_of(stream_key, extent, pieces, -0.22, 0.18)
    return jnp.clip(spiked(drawn, jax.random.fold_in(stream_key, 3), *heavy), -most, most).astype(kind)


def setup_inputs(seed: int = 0) -> dict:
    key_of = jax.random.split(jax.random.key(seed), 9)
    return {
        "draft_q": draw_draft_q(jax.random.fold_in(key_of[8], 71), 0),
        "draft_kv": bell_draw(key_of[1], (2, ROWS, WIDTH), 1.0, 6.0, ((1, 8), (2, 4))),
        "kv_pool": draw_kv_pool(jax.random.fold_in(key_of[8], 71), 0),
        "page_table": draw_page_table(jax.random.fold_in(key_of[8], 71), 0),
        "cache_len": draw_cache_len(jax.random.fold_in(key_of[8], 71), 0),
        "tree_mask": draw_tree_mask(jax.random.fold_in(key_of[8], 71), 0),
        "accepted_rows": draw_accepted_rows(jax.random.fold_in(key_of[8], 71), 0),
        "out_weight": heavy_noise(key_of[7], (WIDTH, D), WIDTH ** -0.5, 0.125, ((0, 4),), (0, 1, 4, 2.0)),
    }


NEGATIVE = -1e+30

def block_stats(scores, allowed):
    masked = jnp.where(allowed, scores, NEGATIVE)
    block_max = lax.optimization_barrier(jnp.max(masked, axis=-1))
    weights = jnp.where(allowed, jnp.exp(masked - block_max[..., None]), 0.0)
    block_total = lax.optimization_barrier(jnp.sum(weights, axis=-1))
    rounded = lax.optimization_barrier(weights.astype(jnp.bfloat16)).astype(jnp.float32)
    return (block_max, block_total, rounded)

def reference(draft_q, draft_kv, kv_pool, page_table, cache_len, tree_mask, accepted_rows, out_weight):
    inv_root = 1.0 / math.sqrt(HD)
    highest = lax.Precision.HIGHEST

    def one_request(request):
        queries = lax.dynamic_slice_in_dim(draft_q, request * DRAFT, DRAFT, 0).astype(jnp.float32).reshape(DRAFT, HEADS, HD)
        slot_row = lax.dynamic_index_in_dim(page_table, request, 0, keepdims=False)
        safe_slots = jnp.maximum(slot_row, 0)
        page_keys = kv_pool[0][safe_slots].astype(jnp.float32).reshape(MAXP, PAGE, HEADS, HD)
        page_values = kv_pool[1][safe_slots].astype(jnp.float32).reshape(MAXP, PAGE, HEADS, HD)
        length = lax.dynamic_index_in_dim(cache_len, request, 0, keepdims=False)
        positions = jnp.arange(MAXP)[:, None] * PAGE + jnp.arange(PAGE)[None, :]
        is_live = (slot_row[:, None] >= 0) & (positions < length)
        scores = jnp.einsum('qhd,pthd->phqt', queries, page_keys, precision=highest) * inv_root
        page_max, page_total, page_weight = block_stats(scores, is_live[:, None, None, :])
        page_out = jnp.einsum('phqt,pthd->phqd', page_weight, page_values, precision=highest)
        draft_keys = lax.dynamic_slice_in_dim(draft_kv[0], request * DRAFT, DRAFT, 0).astype(jnp.float32).reshape(DRAFT, HEADS, HD)
        draft_values = lax.dynamic_slice_in_dim(draft_kv[1], request * DRAFT, DRAFT, 0).astype(jnp.float32).reshape(DRAFT, HEADS, HD)
        mask_rows = lax.dynamic_index_in_dim(tree_mask, request, 0, keepdims=False) == 1
        tree_scores = jnp.einsum('qhd,khd->hqk', queries, draft_keys, precision=highest) * inv_root
        tree_max, tree_total, tree_weight = block_stats(tree_scores, mask_rows[None, :, :])
        tree_out = jnp.einsum('hqk,khd->hqd', tree_weight, draft_values, precision=highest)
        row_top = jnp.maximum(lax.optimization_barrier(jnp.max(page_max, axis=0)), tree_max)
        page_factor = jnp.exp(page_max - row_top[None])
        tree_factor = jnp.exp(tree_max - row_top)
        numerator = lax.optimization_barrier(jnp.sum(page_factor[..., None] * page_out, axis=0)) + tree_factor[..., None] * tree_out
        denominator = lax.optimization_barrier(jnp.sum(page_factor * page_total, axis=0)) + tree_factor * tree_total
        attention = numerator / denominator[..., None]
        return jnp.transpose(attention, (1, 0, 2)).reshape(DRAFT, WIDTH).astype(jnp.bfloat16)
    attention_all = lax.map(one_request, jnp.arange(REQ)).reshape(ROWS, WIDTH)
    layer_out = jnp.dot(attention_all, out_weight, preferred_element_type=jnp.float32).astype(jnp.bfloat16)
    padded = jnp.concatenate([accepted_rows.astype(jnp.int32), jnp.full((REQ, PAGE - DRAFT), -1, jnp.int32)], axis=1)
    onehot = (padded[:, :, None] == jnp.arange(DRAFT).astype(jnp.int32)[None, None, :]).astype(jnp.float32)
    blocks = draft_kv.astype(jnp.float32).reshape(2, REQ, DRAFT, WIDTH)
    accepted_kv = jnp.einsum('rji,crid->crjd', onehot, blocks, precision=highest).astype(jnp.bfloat16)
    return (layer_out, accepted_kv)
```

```python
import functools
import math

import jax
import jax.numpy as jnp
from jax import lax
from jax.experimental import pallas as pl
from jax.experimental.pallas import tpu as pltpu
from jax.sharding import PartitionSpec as P

HD = 128
CHUNKS = 2
UNROLL = 8
LOADS = 4
THIRD = 32
NEGATIVE = -1e30
TINY = 1e-30
MESH = pl.DeviceIdType.MESH
ANY = pl.BlockSpec(memory_space=pl.ANY)
VMEM = pl.BlockSpec(memory_space=pltpu.VMEM)
NT = (((1,), (1,)), ((), ()))
NN = (((1,), (0,)), ((), ()))
TN = (((0,), (0,)), ((), ()))
F32 = jnp.float32
BF16 = jnp.bfloat16


def with_stats(lse):
    lane = lax.broadcasted_iota(jnp.int32, lse.shape, 1)
    high = lse.astype(BF16).astype(F32)
    rest = lse - high
    mid = rest.astype(BF16).astype(F32)
    low = rest - mid
    return jnp.where(lane < THIRD, high, jnp.where(lane < 2 * THIRD, mid, low)).astype(BF16)


def stats_of(terms):
    x = terms.astype(F32)
    return x + pltpu.roll(x, HD - THIRD, 1) + pltpu.roll(x, HD - 2 * THIRD, 1)


def fused_kernel(n_req, n_pages, n_seq, n_tp, group, table_in, len_in, mask_in, accepted_in, q, kv, pool, weight,
                 out, acc_kv, *scratch):
    C = CHUNKS
    qa = scratch[:C]
    kva = scratch[C:C + 2]
    snd1 = scratch[C + 2:2 * C + 2]
    rcv1 = scratch[2 * C + 2:3 * C + 2]
    snd2 = scratch[3 * C + 2:4 * C + 2]
    rcv2 = scratch[4 * C + 2:5 * C + 2]
    (table, cache_len, mask, accepted, picked, zeros, kbuf, vbuf, wq, xs, m_row, l_row, m_top, l_sum, column, acc_st,
     fin_m, fin_l, fin_a, tree_m, tree_l, tree_a, wbuf, att, proj, pbuf, prbuf,
     req, left, prev, last,
     tsem, qsem, qrsem, fsem, osem_q, xsem, xrsem, asem, arsem, cfsem, okvsem,
     ksem, vsem, wsem, s1sem, s1rsem, s2sem, s2rsem, psem, prsem, zsem, osem) = scratch[5 * C + 2:]
    me = lax.axis_index("seq")
    tp = lax.axis_index("tp")
    grp = me // group
    inner = lax.rem(me, group)
    n_slots, page_len, width = kbuf.shape
    rows, cw = qa[0].shape[1:]
    n_draft = rows * group
    heads = width // HD
    hc = heads // C
    out_w = out.shape[1]
    scale = 1.0 / math.sqrt(HD)

    def across(d):
        return lax.rem(grp + d, n_req) * group + inner

    def other(d):
        return grp * group + lax.rem(inner + d, group)

    def remote(a, b, s, r, where):
        return pltpu.make_async_remote_copy(
            src_ref=a, dst_ref=b, send_sem=s, recv_sem=r, device_id=where, device_id_type=MESH)

    sent = []

    def send(*args):
        c = remote(*args)
        c.start()
        sent.append(c)

    def start(a, b, s):
        c = pltpu.make_async_copy(a, b, s)
        c.start()
        return c

    def cols(c):
        return pl.ds(c * cw, cw)

    barrier = pltpu.get_barrier_semaphore()
    for d in range(1, n_req):
        pl.semaphore_signal(barrier, inc=1, device_id={"seq": across(d)}, device_id_type=MESH)
    for d in range(1, group):
        pl.semaphore_signal(barrier, inc=1, device_id={"seq": other(d)}, device_id_type=MESH)
    for d in range(1, n_tp):
        pl.semaphore_signal(barrier, inc=1, device_id={"tp": lax.rem(tp + d, n_tp)}, device_id_type=MESH)
    tables = [start(table_in, table, tsem.at[0]), start(len_in, cache_len, tsem.at[1]),
              start(mask_in.at[me], mask, tsem.at[2]), start(accepted_in, accepted, tsem.at[3])]
    own_q = [start(q.at[:, cols(c)], qa[c].at[me], osem_q.at[c]) for c in range(C)]
    own_kv = [start(kv.at[i], kva[i].at[me], okvsem.at[i]) for i in range(2)]
    pl.semaphore_wait(barrier, n_req + group + n_tp - 3)

    for c in range(C):
        for d in range(n_req - 1, 0, -1):
            send(q.at[:, cols(c)], qa[c].at[me], qsem.at[c, d - 1], qrsem.at[c, me], {"seq": across(d)})
        for d in range(1, group):
            send(q.at[:, cols(c)], qa[c].at[me], qsem.at[c, n_req - 2 + d], qrsem.at[c, me], {"seq": other(d)})
    for i in range(2):
        for d in range(1, group):
            send(kv.at[i], kva[i].at[me], xsem.at[i, d - 1], arsem.at[i, me], {"seq": other(d)})

    for i in range(2):
        for d in range(n_req - 1, 0, -1):
            send(kv.at[i], kva[i].at[me], asem.at[i, d - 1], arsem.at[i, me], {"seq": across(d)})

    n_load = min(LOADS, n_slots)
    per = n_slots // n_load
    pool_loads = []
    for i in range(n_load):
        at = pl.ds(i * per, per)
        pool_loads.append(start(pool.at[0, at], kbuf.at[at], ksem.at[i]))
        pool_loads.append(start(pool.at[1, at], vbuf.at[at], vsem.at[i]))
    w_loads = [start(weight.at[:, pl.ds(t * out_w, out_w)], wbuf.at[t], wsem.at[t]) for t in range(n_tp)]

    acc_st[0] = jnp.zeros(acc_st.shape[1:], F32)
    zeros[...] = jnp.zeros(zeros.shape, zeros.dtype)
    writes = []
    for r in range(n_req):
        for i in range(2):
            writes.append(start(zeros, acc_kv.at[i, r, pl.ds(n_draft, zeros.shape[0])], zsem.at[r, i]))
    for c in tables:
        c.wait()
    shape = table.shape
    index = (lax.broadcasted_iota(jnp.int32, shape, 0) * n_pages + lax.broadcasted_iota(jnp.int32, shape, 1) + 1)
    slots = table[...]
    for r in range(n_req):
        last[r] = 0
    for s in range(n_slots):
        number = jnp.sum(jnp.where(slots == me * n_slots + s, index, 0))
        place = jnp.maximum(number - 1, 0)
        r = jnp.minimum(lax.div(place, n_pages), n_req - 1)
        n = jnp.where(number > 0, cache_len[r] - (place - r * n_pages) * page_len, 0)
        req[s] = r
        left[s] = n
        prev[s] = last[r]
        for i in range(n_req):
            last[i] = jnp.where((n > 0) & (r == i), s + 1, last[i])

    def q_arrived(c, b):
        remote(qa[c].at[b], qa[c].at[b], qsem.at[c, 0], qrsem.at[c, b], {"seq": other(1)}).wait_recv()

    def kv_arrived(i, b):
        remote(kva[i].at[b], kva[i].at[b], asem.at[i, 0], arsem.at[i, b], {"seq": other(1)}).wait_recv()

    def q_forward(c):
        for e in range(1, n_req):
            b = across(e)
            q_arrived(c, b)
            for d in range(1, group):
                send(qa[c].at[b], qa[c].at[b], fsem.at[c, e - 1, d - 1], qrsem.at[c, b], {"seq": other(d)})

    def kv_forward(i):
        for e in range(1, n_req):
            b = across(e)
            kv_arrived(i, b)
            for d in range(1, group):
                send(kva[i].at[b], kva[i].at[b], cfsem.at[i, e - 1, d - 1], arsem.at[i, b], {"seq": other(d)})

    def q_wait(c):
        for d in range(1, group):
            q_arrived(c, other(d))
            for e in range(1, n_req):
                q_arrived(c, lax.rem(grp + e, n_req) * group + lax.rem(inner + d, group))

    def tree():
        for c in range(C):
            own_q[c].wait()
        for i in range(2):
            own_kv[i].wait()
            for d in range(1, group):
                kv_arrived(i, other(d))
        allowed = mask[...] == 1
        for h in range(heads):
            c, at = h // hc, slice(h % hc * HD, (h % hc + 1) * HD)
            full = slice(h * HD, (h + 1) * HD)
            keys = jnp.concatenate([kva[0][grp * group + g, :, full] for g in range(group)], axis=0)
            values = jnp.concatenate([kva[1][grp * group + g, :, full] for g in range(group)], axis=0)
            x = lax.dot_general(qa[c][me, :, at], keys, NT, preferred_element_type=F32) * scale
            x = jnp.where(allowed, x, NEGATIVE)
            top = jnp.max(x, axis=1, keepdims=True)
            p = jnp.where(allowed, jnp.exp(x - top), 0.0)
            tree_m[h] = jnp.broadcast_to(top, (rows, HD))
            tree_l[h] = jnp.broadcast_to(jnp.sum(p, axis=1, keepdims=True), (rows, HD))
            tree_a[:, full] = jnp.dot(p.astype(BF16), values, preferred_element_type=F32)

    def attend(c):
        blank = jnp.zeros((n_draft, HD), F32)
        for r in range(n_req):
            for k in range(hc // 2):
                for i in range(2):
                    at = slice((2 * k + i) * HD, (2 * k + i + 1) * HD)
                    query = jnp.concatenate([qa[c][r * group + g, :, at] for g in range(group)], axis=0).astype(F32)
                    both = [query, blank] if i == 0 else [blank, query]
                    wq[r, k, i * HD:(i + 1) * HD] = jnp.concatenate(both, axis=0).T.astype(BF16)

        def score(s, carry):
            r = req[s]
            live = lax.broadcasted_iota(jnp.int32, (page_len, HD), 0) < left[s]
            for k in range(hc // 2):
                full = slice(c * cw + 2 * k * HD, c * cw + (2 * k + 2) * HD)
                x = jnp.dot(kbuf[s, :, full], wq[r, k], preferred_element_type=F32)
                x = jnp.where(live, x * scale, NEGATIVE)
                xs[s, k] = x
                m_row[s, k] = jnp.broadcast_to(jnp.max(x, axis=0, keepdims=True), (8, HD))
            return carry

        lax.fori_loop(0, n_slots, score, 0, unroll=min(UNROLL, n_slots))
        for k in range(hc // 2):
            tops = [jnp.full((8, HD), NEGATIVE, F32)] * n_req
            for s in range(n_slots):
                page = m_row[s, k]
                for r in range(n_req):
                    mine = (req[s] == r) & (left[s] > 0)
                    tops[r] = jnp.where(mine, jnp.maximum(tops[r], page), tops[r])
            for r in range(n_req):
                m_top[r, k] = tops[r]

        def weigh(s, carry):
            r = req[s]
            before = prev[s]
            for k in range(hc // 2):
                p = jnp.exp(xs[s, k] - m_top[r, k, 0:1])
                l_row[s, k] = jnp.broadcast_to(jnp.sum(p, axis=0, keepdims=True), (8, HD))
                p = p.T.astype(BF16)
                for i in range(2):
                    h = 2 * k + i
                    at = slice(h * HD, (h + 1) * HD)
                    full = slice(c * cw + h * HD, c * cw + (h + 1) * HD)
                    o = jnp.dot(p[i * n_draft:(i + 1) * n_draft], vbuf[s, :, full], preferred_element_type=F32)
                    acc_st[s + 1, :, at] = acc_st[before, :, at] + o
            return carry

        lax.fori_loop(0, n_slots, weigh, 0, unroll=min(UNROLL, n_slots))
        sub = lax.broadcasted_iota(jnp.int32, (8, HD), 0)
        for k in range(hc // 2):
            sums = [jnp.zeros((8, HD), F32)] * n_req
            for s in range(n_slots):
                page = l_row[s, k]
                for r in range(n_req):
                    mine = (req[s] == r) & (left[s] > 0)
                    sums[r] = jnp.where(mine, sums[r] + page, sums[r])
            for r in range(n_req):
                l_sum[r, k] = sums[r]
            tiles = []
            for half in range(-(-n_req // 4)):
                tile = jnp.zeros((8, HD), F32)
                for d in range(4 * half, min(4 * half + 4, n_req)):
                    r = lax.rem(grp + d, n_req)
                    tile = jnp.where(sub == 2 * (d % 4), m_top[r, k], tile)
                    tile = jnp.where(sub == 2 * (d % 4) + 1, l_sum[r, k], tile)
                tiles.append(tile)
            tiles += [jnp.zeros((8, HD), F32)] * (HD // 8 - len(tiles))
            column[c, k] = jnp.concatenate(tiles, axis=0).T

    def stat(c, d, h, j):
        mine = pl.ds(pl.multiple_of(h % 2 * n_draft + j * rows, rows), rows)
        both = column[c, h // 2, mine]
        shape = (rows, HD)
        return (jnp.broadcast_to(both[:, 2 * d:2 * d + 1], shape), jnp.broadcast_to(both[:, 2 * d + 1:2 * d + 2], shape))

    lane = lax.rem(lax.broadcasted_iota(jnp.int32, (rows, HD), 1), THIRD)
    order = list(range(n_req - 1, -1, -1))

    def piece(d, j):
        at = last[lax.rem(grp + d, n_req)]
        mine = pl.ds(pl.multiple_of(j * rows, rows), rows)
        return at, mine

    def pack(c):
        for d in order:
            for e in range(1, group):
                j = lax.rem(inner + e, group)
                at, mine = piece(d, j)
                info = jnp.zeros((rows, HD), F32)
                for h in range(hc):
                    top, total = stat(c, d, h, j)
                    total = jnp.maximum(total, TINY)
                    part = slice(h * HD, (h + 1) * HD)
                    snd1[c][d, e - 1, :, part] = (acc_st[at, mine, part] / total).astype(BF16)
                    info = jnp.where(lane == h, top + jnp.log(total), info)
                snd1[c][d, e - 1, :, cw:] = with_stats(info)
                send(snd1[c].at[d, e - 1], rcv1[c].at[d, e - 1], s1sem.at[c, d, e - 1], s1rsem.at[c, d, e - 1],
                     {"seq": other(e)})
        for d in order:
            at, mine = piece(d, inner)
            fin_a[c, d] = acc_st[at, mine]

    def merge(c):
        for d in order:
            infos = []
            for e in range(1, group):
                remote(snd1[c].at[d, e - 1], rcv1[c].at[d, e - 1], s1sem.at[c, d, e - 1], s1rsem.at[c, d, e - 1],
                       {"seq": other(e)}).wait_recv()
                infos.append(stats_of(rcv1[c][d, e - 1, :, cw:]))
            packed = jnp.zeros((rows, HD), F32)
            for h in range(hc):
                part = slice(h * HD, (h + 1) * HD)
                own, mass = stat(c, d, h, inner)
                top = own
                for info in infos:
                    top = jnp.maximum(top, info[:, h:h + 1])
                f = jnp.exp(own - top)
                den = f * mass
                num = f * fin_a[c, d, :, part]
                for e, info in enumerate(infos):
                    f = jnp.exp(info[:, h:h + 1] - top)
                    den = den + f
                    num = num + f * rcv1[c][d, e, :, part].astype(F32)
                if d > 0:
                    den = jnp.maximum(den, TINY)
                    snd2[c][d - 1, :, part] = (num / den).astype(BF16)
                    packed = jnp.where(lane == h, top + jnp.log(den), packed)
                else:
                    fin_m[c, h] = top
                    fin_l[c, h] = den
                    fin_a[c, 0, :, part] = num
            if d > 0:
                snd2[c][d - 1, :, cw:] = with_stats(packed)
                send(snd2[c].at[d - 1], rcv2[c].at[d - 1], s2sem.at[c, d - 1], s2rsem.at[c, d - 1],
                     {"seq": across(d)})

    def finish(c):
        infos = []
        for d in range(1, n_req):
            remote(snd2[c].at[d - 1], rcv2[c].at[d - 1], s2sem.at[c, d - 1], s2rsem.at[c, d - 1],
                   {"seq": across(d)}).wait_recv()
            infos.append(stats_of(rcv2[c][d - 1, :, cw:]))
        for h in range(hc):
            part = slice(h * HD, (h + 1) * HD)
            full = slice(c * cw + h * HD, c * cw + (h + 1) * HD)
            top = jnp.maximum(fin_m[c, h], tree_m[c * hc + h])
            for info in infos:
                top = jnp.maximum(top, info[:, h:h + 1])
            f = jnp.exp(fin_m[c, h] - top)
            g = jnp.exp(tree_m[c * hc + h] - top)
            den = f * fin_l[c, h] + g * tree_l[c * hc + h]
            num = f * fin_a[c, 0, :, part] + g * tree_a[:, full]
            for d, info in enumerate(infos):
                f = jnp.exp(info[:, h:h + 1] - top)
                den = den + f
                num = num + f * rcv2[c][d, :, part].astype(F32)
            att[:, full] = (num / den).astype(BF16)

    for c in range(C):
        q_forward(c)
        if c == 0:
            tree()
    for c in pool_loads:
        c.wait()
    for c in range(C):
        q_wait(c)
        attend(c)
        pack(c)
    merge(0)
    for c in range(1, C):
        merge(c)
    kv_forward(0)
    kv_forward(1)
    for c in w_loads:
        c.wait()
    for c in range(C - 1):
        finish(c)
        for t in range(n_tp):
            term = jnp.dot(att[:, c * cw:(c + 1) * cw], wbuf[t, c * cw:(c + 1) * cw], preferred_element_type=F32)
            proj[t] = term if c == 0 else proj[t] + term
    finish(C - 1)
    tail = slice((C - 1) * cw, C * cw)
    for d in range(1, n_tp):
        peer = lax.rem(tp + d, n_tp)
        pbuf[d - 1] = (proj[peer] + jnp.dot(att[:, tail], wbuf[peer, tail],
                                            preferred_element_type=F32)).astype(BF16)
        send(pbuf.at[d - 1], prbuf.at[d - 1], psem.at[d - 1], prsem.at[d - 1], {"tp": peer})
    total = proj[tp] + jnp.dot(att[:, tail], wbuf[tp, tail], preferred_element_type=F32)
    for i in range(2):
        for d in range(1, group):
            for e in range(1, n_req):
                kv_arrived(i, lax.rem(grp + e, n_req) * group + lax.rem(inner + d, group))
        for r in range(n_req):
            pick = (lax.broadcasted_iota(jnp.int32, (n_draft, n_draft), 0) == accepted[r:r + 1, :]).astype(BF16)
            blocks = jnp.concatenate([kva[i][r * group + g] for g in range(group)], axis=0)
            picked[r, i] = lax.dot_general(pick, blocks, TN, preferred_element_type=F32).astype(BF16)
            writes.append(start(picked.at[r, i], acc_kv.at[i, r, pl.ds(0, n_draft)], osem.at[r, i]))
    for d in range(1, n_tp):
        remote(pbuf.at[d - 1], prbuf.at[d - 1], psem.at[d - 1], prsem.at[d - 1],
               {"tp": lax.rem(tp + d, n_tp)}).wait_recv()
        total = total + prbuf[d - 1].astype(F32)
    out[...] = total.astype(out.dtype)
    for c in writes:
        c.wait()
    for c in sent:
        c.wait_send()


def copy_kernel(accepted, layer, out, layer_out, held, held_layer, isem, osem):
    halves, n_req = accepted.shape[:2]
    parts = [(layer, held_layer, layer_out)]
    for c in range(halves):
        for r in range(n_req):
            parts.append((accepted.at[c, r], held.at[c, r], out.at[c, r]))
    loads = [pltpu.make_async_copy(a, b, isem.at[i]) for i, (a, b, _) in enumerate(parts)]
    stores = [pltpu.make_async_copy(b, c, osem.at[i]) for i, (_, b, c) in enumerate(parts)]
    for c in loads:
        c.start()
    for load, store in zip(loads, stores):
        load.wait()
        store.start()
    for c in stores:
        c.wait()


def body(draft_q, draft_kv, kv_pool, page_table, cache_len, tree_mask, accepted_rows, out_weight):
    n_seq = lax.axis_size("seq")
    n_tp = lax.axis_size("tp")
    rows, width = draft_q.shape
    heads = width // HD
    n_req, n_pages = page_table.shape
    n_draft = tree_mask.shape[1]
    n_slots, page_len = kv_pool.shape[1:3]
    group = n_seq // n_req
    out_w = out_weight.shape[1] // n_tp
    C = CHUNKS
    cw = width // C
    hc = heads // C
    dma = pltpu.SemaphoreType.DMA
    vm = pltpu.VMEM
    smem = pltpu.SMEM

    layer, accepted_block = pl.pallas_call(
        functools.partial(fused_kernel, n_req, n_pages, n_seq, n_tp, group),
        out_shape=(jax.ShapeDtypeStruct((rows, out_w), BF16),
                   jax.ShapeDtypeStruct((2, n_req, page_len, width), BF16)),
        in_specs=[ANY] * 8,
        out_specs=(VMEM, ANY),
        scratch_shapes=[vm((n_seq, rows, cw), BF16)] * C + [vm((n_seq, rows, width), BF16)] * 2
        + [vm((n_req, group - 1, rows, cw + HD), BF16)] * (2 * C)
        + [vm((n_req - 1, rows, cw + HD), BF16)] * (2 * C)
        + [vm(page_table.shape, jnp.int32), smem((n_req,), jnp.int32), vm((rows, n_draft), jnp.int32),
           vm(accepted_rows.shape, jnp.int32),
           vm((n_req, 2, n_draft, width), BF16), vm((page_len - n_draft, width), BF16),
           vm((n_slots, page_len, width), BF16), vm((n_slots, page_len, width), BF16),
           vm((n_req, hc // 2, 2 * HD, HD), BF16), vm((n_slots, hc // 2, page_len, HD), F32),
           vm((n_slots, hc // 2, 8, HD), F32), vm((n_slots, hc // 2, 8, HD), F32),
           vm((n_req, hc // 2, 8, HD), F32), vm((n_req, hc // 2, 8, HD), F32), vm((C, hc // 2, HD, HD), F32),
           vm((n_slots + 1, n_draft, cw), F32),
           vm((C, hc, rows, HD), F32), vm((C, hc, rows, HD), F32), vm((C, n_req, rows, cw), F32),
           vm((heads, rows, HD), F32), vm((heads, rows, HD), F32), vm((rows, width), F32),
           vm((n_tp, width, out_w), BF16), vm((rows, width), BF16), vm((n_tp, rows, out_w), F32),
           vm((n_tp - 1, rows, out_w), BF16), vm((n_tp - 1, rows, out_w), BF16),
           smem((n_slots,), jnp.int32), smem((n_slots,), jnp.int32), smem((n_slots,), jnp.int32),
           smem((n_req,), jnp.int32),
           dma((4,)), dma((C, n_req + group - 2)), dma((C, n_seq)), dma((C, n_req - 1, group - 1)), dma((C,)),
           dma((2, group - 1)), dma((1,)), dma((2, n_req - 1)), dma((2, n_seq)),
           dma((2, n_req - 1, group - 1)), dma((2,)),
           dma((LOADS,)), dma((LOADS,)), dma((n_tp,)),
           dma((C, n_req, group - 1)), dma((C, n_req, group - 1)), dma((C, n_req - 1)), dma((C, n_req - 1)),
           dma((n_tp - 1,)), dma((n_tp - 1,)), dma((n_req, 2)), dma((n_req, 2))],
        compiler_params=pltpu.CompilerParams(collective_id=0, has_side_effects=True,
                                             vmem_limit_bytes=58 << 20),
        cost_estimate=pl.CostEstimate(flops=10 ** 10, bytes_accessed=3 * 10 ** 7,
                                      transcendentals=10 ** 6),
    )(page_table, cache_len, tree_mask.reshape(n_seq, rows, n_draft), accepted_rows, draft_q, draft_kv, kv_pool,
      out_weight)

    accepted_kv, layer_out = pl.pallas_call(
        copy_kernel,
        out_shape=(jax.ShapeDtypeStruct((2, n_req, page_len, width), BF16),
                   jax.ShapeDtypeStruct((rows, out_w), BF16)),
        in_specs=[ANY, ANY],
        out_specs=(ANY, ANY),
        scratch_shapes=[vm((2, n_req, page_len, width), BF16), vm((rows, out_w), BF16),
                        dma((2 * n_req + 1,)), dma((2 * n_req + 1,))],
        compiler_params=pltpu.CompilerParams(vmem_limit_bytes=58 << 20),
    )(accepted_block, layer)
    return (layer_out, accepted_kv)


def solution(mesh):
    return jax.shard_map(
        body,
        mesh=mesh,
        in_specs=(P("seq", "tp"), P(None, "seq", "tp"), P(None, "seq", None, "tp"),
                  P(), P(), P(), P(), P("tp", None)),
        out_specs=(P("seq", "tp"), P(None, None, None, "tp")),
        check_vma=False,
    )
```

```python
import functools
import math

import jax
import jax.numpy as jnp
from jax import lax
from jax.experimental import pallas as pl
from jax.experimental.pallas import tpu as pltpu
from jax.sharding import PartitionSpec as P

HD = 128
CHUNKS = 2
UNROLL = 8
LOADS = 4
THIRD = 32
NEGATIVE = -1e30
TINY = 1e-30
MESH = pl.DeviceIdType.MESH
ANY = pl.BlockSpec(memory_space=pl.ANY)
VMEM = pl.BlockSpec(memory_space=pltpu.VMEM)
NT = (((1,), (1,)), ((), ()))
NN = (((1,), (0,)), ((), ()))
TN = (((0,), (0,)), ((), ()))
F32 = jnp.float32
BF16 = jnp.bfloat16


def with_stats(lse):
    lane = lax.broadcasted_iota(jnp.int32, lse.shape, 1)
    high = lse.astype(BF16).astype(F32)
    rest = lse - high
    mid = rest.astype(BF16).astype(F32)
    low = rest - mid
    return jnp.where(lane < THIRD, high, jnp.where(lane < 2 * THIRD, mid, low)).astype(BF16)


def stats_of(terms):
    x = terms.astype(F32)
    return x + pltpu.roll(x, HD - THIRD, 1) + pltpu.roll(x, HD - 2 * THIRD, 1)


def fused_kernel(n_req, n_pages, n_seq, n_tp, group, table_in, len_in, mask_in, accepted_in, q, kv, pool, weight,
                 out, acc_kv, *scratch):
    C = CHUNKS
    qa = scratch[:C]
    kva = scratch[C:C + 2]
    snd1 = scratch[C + 2:2 * C + 2]
    rcv1 = scratch[2 * C + 2:3 * C + 2]
    snd2 = scratch[3 * C + 2:4 * C + 2]
    rcv2 = scratch[4 * C + 2:5 * C + 2]
    (table, cache_len, mask, accepted, page, kbuf, vbuf, wq, xs, m_row, l_row, m_top, l_sum, column, acc_st,
     fin_m, fin_l, fin_a, tree_m, tree_l, tree_a, wbuf, att, proj, pbuf, prbuf,
     req, left, prev, last,
     tsem, qsem, qrsem, fsem, osem_q, xsem, arsem, asem, krsem, cfsem, okvsem,
     ksem, vsem, wsem, s1sem, s1rsem, s2sem, s2rsem, psem, prsem, osem) = scratch[5 * C + 2:]
    me = lax.axis_index("seq")
    tp = lax.axis_index("tp")
    grp = me // group
    inner = lax.rem(me, group)
    n_slots, page_len, width = kbuf.shape
    rows, cw = qa[0].shape[1:]
    n_draft = rows * group
    heads = width // HD
    hc = heads // C
    out_w = out.shape[1]
    scale = 1.0 / math.sqrt(HD)

    def across(d):
        return lax.rem(grp + d, n_req) * group + inner

    def other(d):
        return grp * group + lax.rem(inner + d, group)

    def remote(a, b, s, r, where):
        return pltpu.make_async_remote_copy(
            src_ref=a, dst_ref=b, send_sem=s, recv_sem=r, device_id=where, device_id_type=MESH)

    sent = []

    def send(*args):
        c = remote(*args)
        c.start()
        sent.append(c)

    sent_if = []

    def send_if(condition, *args):
        c = remote(*args)
        pl.when(condition)(lambda: c.start())
        sent_if.append((condition, c))

    def start(a, b, s):
        c = pltpu.make_async_copy(a, b, s)
        c.start()
        return c

    def cols(c):
        return pl.ds(c * cw, cw)

    barrier = pltpu.get_barrier_semaphore()
    for d in range(1, n_req):
        pl.semaphore_signal(barrier, inc=1, device_id={"seq": across(d)}, device_id_type=MESH)
    for d in range(1, group):
        pl.semaphore_signal(barrier, inc=1, device_id={"seq": other(d)}, device_id_type=MESH)
    for d in range(1, n_tp):
        pl.semaphore_signal(barrier, inc=1, device_id={"tp": lax.rem(tp + d, n_tp)}, device_id_type=MESH)
    tables = [start(table_in, table, tsem.at[0]), start(len_in, cache_len, tsem.at[1]),
              start(mask_in.at[me], mask, tsem.at[2]), start(accepted_in, accepted, tsem.at[3])]
    own_q = [start(q.at[:, cols(c)], qa[c].at[me], osem_q.at[c]) for c in range(C)]
    own_kv = [start(kv.at[i], kva[i].at[inner], okvsem.at[i]) for i in range(2)]
    pl.semaphore_wait(barrier, n_req + group + n_tp - 3)

    for i in range(2):
        for d in range(1, group):
            send(kv.at[i], kva[i].at[inner], xsem.at[i, d - 1], arsem.at[i, inner], {"seq": other(d)})
    for c in range(C):
        for d in range(n_req - 1, 0, -1):
            send(q.at[:, cols(c)], qa[c].at[me], qsem.at[c, d - 1], qrsem.at[c, me], {"seq": across(d)})
        for d in range(1, group):
            send(q.at[:, cols(c)], qa[c].at[me], qsem.at[c, n_req - 2 + d], qrsem.at[c, me], {"seq": other(d)})

    n_load = min(LOADS, n_slots)
    per = n_slots // n_load
    pool_loads = []
    for i in range(n_load):
        at = pl.ds(i * per, per)
        pool_loads.append(start(pool.at[0, at], kbuf.at[at], ksem.at[i]))
        pool_loads.append(start(pool.at[1, at], vbuf.at[at], vsem.at[i]))
    w_loads = [start(weight.at[:, pl.ds(t * out_w, out_w)], wbuf.at[t], wsem.at[t]) for t in range(n_tp)]

    acc_st[0] = jnp.zeros(acc_st.shape[1:], F32)
    writes = []
    for c in tables:
        c.wait()
    shape = table.shape
    index = (lax.broadcasted_iota(jnp.int32, shape, 0) * n_pages + lax.broadcasted_iota(jnp.int32, shape, 1) + 1)
    slots = table[...]
    for r in range(n_req):
        last[r] = 0
    for s in range(n_slots):
        number = jnp.sum(jnp.where(slots == me * n_slots + s, index, 0))
        place = jnp.maximum(number - 1, 0)
        r = jnp.minimum(lax.div(place, n_pages), n_req - 1)
        n = jnp.where(number > 0, cache_len[r] - (place - r * n_pages) * page_len, 0)
        req[s] = r
        left[s] = n
        prev[s] = last[r]
        for i in range(n_req):
            last[i] = jnp.where((n > 0) & (r == i), s + 1, last[i])

    def q_arrived(c, b):
        remote(qa[c].at[b], qa[c].at[b], qsem.at[c, 0], qrsem.at[c, b], {"seq": other(1)}).wait_recv()

    def page_rows(i, r, j):
        return acc_kv.at[i, r, pl.ds(pl.multiple_of(j * rows, rows), rows)]

    def accept():
        for i in range(2):
            own_kv[i].wait()
            for d in range(1, group):
                j = lax.rem(inner + d, group)
                remote(kva[i].at[j], kva[i].at[j], xsem.at[i, 0], arsem.at[i, j], {"seq": other(d)}).wait_recv()
        pick = (lax.broadcasted_iota(jnp.int32, (n_draft, n_draft), 0) == accepted[pl.ds(grp, 1), :]).astype(BF16)
        for i in range(2):
            blocks = jnp.concatenate([kva[i][g] for g in range(group)], axis=0)
            page[i] = lax.dot_general(pick, blocks, TN, preferred_element_type=F32).astype(BF16)
            writes.append(start(page.at[i], acc_kv.at[i, grp], osem.at[i]))
            mine = page.at[i, pl.ds(pl.multiple_of(inner * rows, rows), rows)]
            for side in range(2):
                ahead, to = onward(side)
                send_if(ahead, mine, page_rows(i, grp, inner), asem.at[i, side, 0], krsem.at[i, side, 0, 0], to)

    def onward(side):
        if side == 0:
            return grp + 1 < n_req, {"seq": jnp.minimum(grp + 1, n_req - 1) * group + inner}
        return grp > 0, {"seq": jnp.maximum(grp - 1, 0) * group + inner}

    def source(side, k):
        if side == 0:
            return grp >= k, jnp.maximum(grp - k, 0)
        return grp + k < n_req, jnp.minimum(grp + k, n_req - 1)

    def page_arrived(i, k, e):
        for side in range(2):
            there, r = source(side, k)
            at = page_rows(i, r, lax.rem(inner + group - e, group))
            c = remote(at, at, asem.at[i, 0, 0], krsem.at[i, side, k - 1, e], {"seq": other(1)})
            pl.when(there)(lambda c=c: c.wait_recv())

    def page_onward(i, k):
        page_arrived(i, k, 0)
        if k < n_req - 1:
            for side in range(2):
                there, r = source(side, k)
                ahead, to = onward(side)
                at = page_rows(i, r, inner)
                send_if(there & ahead, at, at, asem.at[i, side, k], krsem.at[i, side, k, 0], to)

    def page_spread(i, k):
        for side in range(2):
            there, r = source(side, k)
            at = page_rows(i, r, inner)
            for e in range(1, group):
                send_if(there, at, at, cfsem.at[i, side, k - 1, e - 1], krsem.at[i, side, k - 1, e], {"seq": other(e)})

    def q_forward(c):
        for e in range(1, n_req):
            b = across(e)
            q_arrived(c, b)
            for d in range(1, group):
                send(qa[c].at[b], qa[c].at[b], fsem.at[c, e - 1, d - 1], qrsem.at[c, b], {"seq": other(d)})

    def q_wait(c):
        for d in range(1, group):
            q_arrived(c, other(d))
            for e in range(1, n_req):
                q_arrived(c, lax.rem(grp + e, n_req) * group + lax.rem(inner + d, group))

    def tree():
        for c in range(C):
            own_q[c].wait()
        allowed = mask[...] == 1
        for h in range(heads):
            c, at = h // hc, slice(h % hc * HD, (h % hc + 1) * HD)
            full = slice(h * HD, (h + 1) * HD)
            keys = jnp.concatenate([kva[0][g, :, full] for g in range(group)], axis=0)
            values = jnp.concatenate([kva[1][g, :, full] for g in range(group)], axis=0)
            x = lax.dot_general(qa[c][me, :, at], keys, NT, preferred_element_type=F32) * scale
            x = jnp.where(allowed, x, NEGATIVE)
            top = jnp.max(x, axis=1, keepdims=True)
            p = jnp.where(allowed, jnp.exp(x - top), 0.0)
            tree_m[h] = jnp.broadcast_to(top, (rows, HD))
            tree_l[h] = jnp.broadcast_to(jnp.sum(p, axis=1, keepdims=True), (rows, HD))
            tree_a[:, full] = jnp.dot(p.astype(BF16), values, preferred_element_type=F32)

    def attend(c):
        blank = jnp.zeros((n_draft, HD), F32)
        for r in range(n_req):
            for k in range(hc // 2):
                for i in range(2):
                    at = slice((2 * k + i) * HD, (2 * k + i + 1) * HD)
                    query = jnp.concatenate([qa[c][r * group + g, :, at] for g in range(group)], axis=0).astype(F32)
                    both = [query, blank] if i == 0 else [blank, query]
                    wq[r, k, i * HD:(i + 1) * HD] = jnp.concatenate(both, axis=0).T.astype(BF16)

        def score(s, carry):
            r = req[s]
            live = lax.broadcasted_iota(jnp.int32, (page_len, HD), 0) < left[s]
            for k in range(hc // 2):
                full = slice(c * cw + 2 * k * HD, c * cw + (2 * k + 2) * HD)
                x = jnp.dot(kbuf[s, :, full], wq[r, k], preferred_element_type=F32)
                x = jnp.where(live, x * scale, NEGATIVE)
                xs[s, k] = x
                m_row[s, k] = jnp.broadcast_to(jnp.max(x, axis=0, keepdims=True), (8, HD))
            return carry

        lax.fori_loop(0, n_slots, score, 0, unroll=min(UNROLL, n_slots))
        for k in range(hc // 2):
            tops = [jnp.full((8, HD), NEGATIVE, F32)] * n_req
            for s in range(n_slots):
                page = m_row[s, k]
                for r in range(n_req):
                    mine = (req[s] == r) & (left[s] > 0)
                    tops[r] = jnp.where(mine, jnp.maximum(tops[r], page), tops[r])
            for r in range(n_req):
                m_top[r, k] = tops[r]

        def weigh(s, carry):
            r = req[s]
            before = prev[s]
            for k in range(hc // 2):
                p = jnp.exp(xs[s, k] - m_top[r, k, 0:1])
                l_row[s, k] = jnp.broadcast_to(jnp.sum(p, axis=0, keepdims=True), (8, HD))
                p = p.T.astype(BF16)
                for i in range(2):
                    h = 2 * k + i
                    at = slice(h * HD, (h + 1) * HD)
                    full = slice(c * cw + h * HD, c * cw + (h + 1) * HD)
                    o = jnp.dot(p[i * n_draft:(i + 1) * n_draft], vbuf[s, :, full], preferred_element_type=F32)
                    acc_st[s + 1, :, at] = acc_st[before, :, at] + o
            return carry

        lax.fori_loop(0, n_slots, weigh, 0, unroll=min(UNROLL, n_slots))
        sub = lax.broadcasted_iota(jnp.int32, (8, HD), 0)
        for k in range(hc // 2):
            sums = [jnp.zeros((8, HD), F32)] * n_req
            for s in range(n_slots):
                page = l_row[s, k]
                for r in range(n_req):
                    mine = (req[s] == r) & (left[s] > 0)
                    sums[r] = jnp.where(mine, sums[r] + page, sums[r])
            for r in range(n_req):
                l_sum[r, k] = sums[r]
            tiles = []
            for half in range(-(-n_req // 4)):
                tile = jnp.zeros((8, HD), F32)
                for d in range(4 * half, min(4 * half + 4, n_req)):
                    r = lax.rem(grp + d, n_req)
                    tile = jnp.where(sub == 2 * (d % 4), m_top[r, k], tile)
                    tile = jnp.where(sub == 2 * (d % 4) + 1, l_sum[r, k], tile)
                tiles.append(tile)
            tiles += [jnp.zeros((8, HD), F32)] * (HD // 8 - len(tiles))
            column[c, k] = jnp.concatenate(tiles, axis=0).T

    def stat(c, d, h, j):
        mine = pl.ds(pl.multiple_of(h % 2 * n_draft + j * rows, rows), rows)
        both = column[c, h // 2, mine]
        shape = (rows, HD)
        return (jnp.broadcast_to(both[:, 2 * d:2 * d + 1], shape), jnp.broadcast_to(both[:, 2 * d + 1:2 * d + 2], shape))

    lane = lax.rem(lax.broadcasted_iota(jnp.int32, (rows, HD), 1), THIRD)
    order = list(range(n_req - 1, -1, -1))

    def piece(d, j):
        at = last[lax.rem(grp + d, n_req)]
        mine = pl.ds(pl.multiple_of(j * rows, rows), rows)
        return at, mine

    def pack(c):
        for d in order:
            for e in range(1, group):
                j = lax.rem(inner + e, group)
                at, mine = piece(d, j)
                info = jnp.zeros((rows, HD), F32)
                for h in range(hc):
                    top, total = stat(c, d, h, j)
                    total = jnp.maximum(total, TINY)
                    part = slice(h * HD, (h + 1) * HD)
                    snd1[c][d, e - 1, :, part] = (acc_st[at, mine, part] / total).astype(BF16)
                    info = jnp.where(lane == h, top + jnp.log(total), info)
                snd1[c][d, e - 1, :, cw:] = with_stats(info)
                send(snd1[c].at[d, e - 1], rcv1[c].at[d, e - 1], s1sem.at[c, d, e - 1], s1rsem.at[c, d, e - 1],
                     {"seq": other(e)})
        for d in order:
            at, mine = piece(d, inner)
            fin_a[c, d] = acc_st[at, mine]

    def merge(c):
        for d in order:
            infos = []
            for e in range(1, group):
                remote(snd1[c].at[d, e - 1], rcv1[c].at[d, e - 1], s1sem.at[c, d, e - 1], s1rsem.at[c, d, e - 1],
                       {"seq": other(e)}).wait_recv()
                infos.append(stats_of(rcv1[c][d, e - 1, :, cw:]))
            packed = jnp.zeros((rows, HD), F32)
            for h in range(hc):
                part = slice(h * HD, (h + 1) * HD)
                own, mass = stat(c, d, h, inner)
                top = own
                for info in infos:
                    top = jnp.maximum(top, info[:, h:h + 1])
                f = jnp.exp(own - top)
                den = f * mass
                num = f * fin_a[c, d, :, part]
                for e, info in enumerate(infos):
                    f = jnp.exp(info[:, h:h + 1] - top)
                    den = den + f
                    num = num + f * rcv1[c][d, e, :, part].astype(F32)
                if d > 0:
                    den = jnp.maximum(den, TINY)
                    snd2[c][d - 1, :, part] = (num / den).astype(BF16)
                    packed = jnp.where(lane == h, top + jnp.log(den), packed)
                else:
                    fin_m[c, h] = top
                    fin_l[c, h] = den
                    fin_a[c, 0, :, part] = num
            if d > 0:
                snd2[c][d - 1, :, cw:] = with_stats(packed)
                send(snd2[c].at[d - 1], rcv2[c].at[d - 1], s2sem.at[c, d - 1], s2rsem.at[c, d - 1],
                     {"seq": across(d)})

    def finish(c):
        infos = []
        for d in range(1, n_req):
            remote(snd2[c].at[d - 1], rcv2[c].at[d - 1], s2sem.at[c, d - 1], s2rsem.at[c, d - 1],
                   {"seq": across(d)}).wait_recv()
            infos.append(stats_of(rcv2[c][d - 1, :, cw:]))
        for h in range(hc):
            part = slice(h * HD, (h + 1) * HD)
            full = slice(c * cw + h * HD, c * cw + (h + 1) * HD)
            top = jnp.maximum(fin_m[c, h], tree_m[c * hc + h])
            for info in infos:
                top = jnp.maximum(top, info[:, h:h + 1])
            f = jnp.exp(fin_m[c, h] - top)
            g = jnp.exp(tree_m[c * hc + h] - top)
            den = f * fin_l[c, h] + g * tree_l[c * hc + h]
            num = f * fin_a[c, 0, :, part] + g * tree_a[:, full]
            for d, info in enumerate(infos):
                f = jnp.exp(info[:, h:h + 1] - top)
                den = den + f
                num = num + f * rcv2[c][d, :, part].astype(F32)
            att[:, full] = (num / den).astype(BF16)

    accept()
    for c in range(C):
        q_forward(c)
        if c == 0:
            tree()
    for c in pool_loads:
        c.wait()
    for c in range(C):
        q_wait(c)
        if c == 0:
            page_onward(0, 1)
            page_onward(1, 1)
        attend(c)
        pack(c)
    page_spread(0, 1)
    page_spread(1, 1)
    for k in range(2, n_req - 1):
        for i in range(2):
            page_onward(i, k)
            page_spread(i, k)
    for c in range(C):
        merge(c)
    for i in range(2):
        page_onward(i, n_req - 1)
        page_spread(i, n_req - 1)
    for c in w_loads:
        c.wait()
    for c in range(C - 1):
        finish(c)
        for t in range(n_tp):
            term = jnp.dot(att[:, c * cw:(c + 1) * cw], wbuf[t, c * cw:(c + 1) * cw], preferred_element_type=F32)
            proj[t] = term if c == 0 else proj[t] + term
    finish(C - 1)
    tail = slice((C - 1) * cw, C * cw)
    y, core = tp // 2, lax.rem(tp, 2)
    peers = [lax.rem(y + a, n_tp // 2) * 2 + lax.rem(core + b, 2) for a in range(n_tp // 2 - 1, -1, -1) for b in range(2)][:-2]
    peers.append(y * 2 + 1 - core)
    for d, peer in enumerate(peers):
        pbuf[d] = (proj[peer] + jnp.dot(att[:, tail], wbuf[peer, tail], preferred_element_type=F32)).astype(BF16)
        send(pbuf.at[d], prbuf.at[d], psem.at[d], prsem.at[d], {"tp": peer})
    total = proj[tp] + jnp.dot(att[:, tail], wbuf[tp, tail], preferred_element_type=F32)
    for d, peer in enumerate(peers):
        remote(pbuf.at[d], prbuf.at[d], psem.at[d], prsem.at[d], {"tp": peer}).wait_recv()
        total = total + prbuf[d].astype(F32)
    out[...] = total.astype(out.dtype)
    for i in range(2):
        for d in range(1, n_req):
            for e in range(1, group):
                page_arrived(i, d, e)
    for c in writes:
        c.wait()
    for c in sent:
        c.wait_send()
    for condition, c in sent_if:
        pl.when(condition)(lambda c=c: c.wait_send())


def copy_kernel(accepted, layer, out, layer_out, held, held_layer, zeros, isem, osem, zsem):
    halves, n_req, n_draft = accepted.shape[:3]
    parts = [(layer, held_layer, layer_out)]
    for c in range(halves):
        for r in range(n_req):
            parts.append((accepted.at[c, r], held.at[c, r], out.at[c, r, pl.ds(0, n_draft)]))
    loads = [pltpu.make_async_copy(a, b, isem.at[i]) for i, (a, b, _) in enumerate(parts)]
    stores = [pltpu.make_async_copy(b, c, osem.at[i]) for i, (_, b, c) in enumerate(parts)]
    for c in loads:
        c.start()
    zeros[...] = jnp.zeros(zeros.shape, zeros.dtype)
    blank = [pltpu.make_async_copy(zeros, out.at[c, r, pl.ds(n_draft, zeros.shape[0])], zsem.at[c, r])
             for c in range(halves) for r in range(n_req)]
    for c in blank:
        c.start()
    for load, store in zip(loads, stores):
        load.wait()
        store.start()
    for c in stores + blank:
        c.wait()


def body(draft_q, draft_kv, kv_pool, page_table, cache_len, tree_mask, accepted_rows, out_weight):
    n_seq = lax.axis_size("seq")
    n_tp = lax.axis_size("tp")
    rows, width = draft_q.shape
    heads = width // HD
    n_req, n_pages = page_table.shape
    n_draft = tree_mask.shape[1]
    n_slots, page_len = kv_pool.shape[1:3]
    group = n_seq // n_req
    out_w = out_weight.shape[1] // n_tp
    C = CHUNKS
    cw = width // C
    hc = heads // C
    dma = pltpu.SemaphoreType.DMA
    vm = pltpu.VMEM
    smem = pltpu.SMEM

    layer, accepted_block = pl.pallas_call(
        functools.partial(fused_kernel, n_req, n_pages, n_seq, n_tp, group),
        out_shape=(jax.ShapeDtypeStruct((rows, out_w), BF16),
                   jax.ShapeDtypeStruct((2, n_req, n_draft, width), BF16)),
        in_specs=[ANY] * 8,
        out_specs=(VMEM, ANY),
        scratch_shapes=[vm((n_seq, rows, cw), BF16)] * C + [vm((group, rows, width), BF16)] * 2
        + [vm((n_req, group - 1, rows, cw + HD), BF16)] * (2 * C)
        + [vm((n_req - 1, rows, cw + HD), BF16)] * (2 * C)
        + [vm(page_table.shape, jnp.int32), smem((n_req,), jnp.int32), vm((rows, n_draft), jnp.int32),
           vm(accepted_rows.shape, jnp.int32),
           vm((2, n_draft, width), BF16),
           vm((n_slots, page_len, width), BF16), vm((n_slots, page_len, width), BF16),
           vm((n_req, hc // 2, 2 * HD, HD), BF16), vm((n_slots, hc // 2, page_len, HD), F32),
           vm((n_slots, hc // 2, 8, HD), F32), vm((n_slots, hc // 2, 8, HD), F32),
           vm((n_req, hc // 2, 8, HD), F32), vm((n_req, hc // 2, 8, HD), F32), vm((C, hc // 2, HD, HD), F32),
           vm((n_slots + 1, n_draft, cw), F32),
           vm((C, hc, rows, HD), F32), vm((C, hc, rows, HD), F32), vm((C, n_req, rows, cw), F32),
           vm((heads, rows, HD), F32), vm((heads, rows, HD), F32), vm((rows, width), F32),
           vm((n_tp, width, out_w), BF16), vm((rows, width), BF16), vm((n_tp, rows, out_w), F32),
           vm((n_tp - 1, rows, out_w), BF16), vm((n_tp - 1, rows, out_w), BF16),
           smem((n_slots,), jnp.int32), smem((n_slots,), jnp.int32), smem((n_slots,), jnp.int32),
           smem((n_req,), jnp.int32),
           dma((4,)), dma((C, n_req + group - 2)), dma((C, n_seq)), dma((C, n_req - 1, group - 1)), dma((C,)),
           dma((2, group - 1)), dma((2, group)), dma((2, 2, n_req - 1)), dma((2, 2, n_req - 1, group)),
           dma((2, 2, n_req - 1, group - 1)), dma((2,)),
           dma((LOADS,)), dma((LOADS,)), dma((n_tp,)),
           dma((C, n_req, group - 1)), dma((C, n_req, group - 1)), dma((C, n_req - 1)), dma((C, n_req - 1)),
           dma((n_tp - 1,)), dma((n_tp - 1,)), dma((2,))],
        compiler_params=pltpu.CompilerParams(collective_id=0, has_side_effects=True,
                                             vmem_limit_bytes=58 << 20),
        cost_estimate=pl.CostEstimate(flops=10 ** 10, bytes_accessed=3 * 10 ** 7,
                                      transcendentals=10 ** 6),
    )(page_table, cache_len, tree_mask.reshape(n_seq, rows, n_draft), accepted_rows, draft_q, draft_kv, kv_pool,
      out_weight)

    accepted_kv, layer_out = pl.pallas_call(
        copy_kernel,
        out_shape=(jax.ShapeDtypeStruct((2, n_req, page_len, width), BF16),
                   jax.ShapeDtypeStruct((rows, out_w), BF16)),
        in_specs=[ANY, ANY],
        out_specs=(ANY, ANY),
        scratch_shapes=[vm((2, n_req, n_draft, width), BF16), vm((rows, out_w), BF16),
                        vm((page_len - n_draft, width), BF16),
                        dma((2 * n_req + 1,)), dma((2 * n_req + 1,)), dma((2, n_req))],
        compiler_params=pltpu.CompilerParams(vmem_limit_bytes=58 << 20),
    )(accepted_block, layer)
    return (layer_out, accepted_kv)


def solution(mesh):
    return jax.shard_map(
        body,
        mesh=mesh,
        in_specs=(P("seq", "tp"), P(None, "seq", "tp"), P(None, "seq", None, "tp"),
                  P(), P(), P(), P(), P("tp", None)),
        out_specs=(P("seq", "tp"), P(None, None, None, "tp")),
        check_vma=False,
    )
```

```python
import functools
import math

import jax
import jax.numpy as jnp
from jax import lax
from jax.experimental import pallas as pl
from jax.experimental.pallas import tpu as pltpu
from jax.sharding import PartitionSpec as P

HD = 128
CHUNKS = 2
UNROLL = 8
LOADS = 4
NEGATIVE = -1e30
MESH = pl.DeviceIdType.MESH
ANY = pl.BlockSpec(memory_space=pl.ANY)
VMEM = pl.BlockSpec(memory_space=pltpu.VMEM)
NT = (((1,), (1,)), ((), ()))
NN = (((1,), (0,)), ((), ()))
TN = (((0,), (0,)), ((), ()))
F32 = jnp.float32
BF16 = jnp.bfloat16


def fused_kernel(n_req, n_pages, n_seq, n_tp, group, table_in, len_in, mask_in, accepted_in, q, kv, pool, weight,
                 out, acc_kv, *scratch):
    C = CHUNKS
    qa = scratch[:C]
    kva = scratch[C:C + 2]
    snd1 = scratch[C + 2:2 * C + 2]
    rcv1 = scratch[2 * C + 2:3 * C + 2]
    snd2 = scratch[3 * C + 2:4 * C + 2]
    rcv2 = scratch[4 * C + 2:5 * C + 2]
    (table, cache_len, mask, accepted, page, kbuf, vbuf, wq, xs, m_row, l_row, m_top, l_sum, column, tile, own_row, their_row, both_row, msg, got, acc_st,
     fin_a, tree_m, tree_l, tree_a, wbuf, att, proj, pbuf, prbuf,
     req, left, prev, last,
     tsem, qsem, qrsem, fsem, osem_q, xsem, arsem, asem, krsem, cfsem, okvsem,
     ksem, vsem, wsem, s1sem, s1rsem, s2sem, s2rsem, psem, prsem, osem,
     t1sem, t1rsem, t2sem, t2rsem) = scratch[5 * C + 2:]
    me = lax.axis_index("seq")
    tp = lax.axis_index("tp")
    grp = me // group
    inner = lax.rem(me, group)
    n_slots, page_len, width = kbuf.shape
    rows, cw = qa[0].shape[1:]
    n_draft = rows * group
    heads = width // HD
    hc = heads // C
    pairs = hc // 2
    lines = n_req * pairs
    out_w = out.shape[1]
    scale = 1.0 / math.sqrt(HD)

    def across(d):
        return lax.rem(grp + d, n_req) * group + inner

    def other(d):
        return grp * group + lax.rem(inner + d, group)

    def remote(a, b, s, r, where):
        return pltpu.make_async_remote_copy(
            src_ref=a, dst_ref=b, send_sem=s, recv_sem=r, device_id=where, device_id_type=MESH)

    sent = []

    def send(*args):
        c = remote(*args)
        c.start()
        sent.append(c)

    sent_if = []

    def send_if(condition, *args):
        c = remote(*args)
        pl.when(condition)(lambda: c.start())
        sent_if.append((condition, c))

    def start(a, b, s):
        c = pltpu.make_async_copy(a, b, s)
        c.start()
        return c

    def cols(c):
        return pl.ds(c * cw, cw)

    barrier = pltpu.get_barrier_semaphore()
    for d in range(1, n_req):
        pl.semaphore_signal(barrier, inc=1, device_id={"seq": across(d)}, device_id_type=MESH)
    for d in range(1, group):
        pl.semaphore_signal(barrier, inc=1, device_id={"seq": other(d)}, device_id_type=MESH)
    for d in range(1, n_tp):
        pl.semaphore_signal(barrier, inc=1, device_id={"tp": lax.rem(tp + d, n_tp)}, device_id_type=MESH)
    tables = [start(table_in, table, tsem.at[0]), start(len_in, cache_len, tsem.at[1]),
              start(mask_in.at[me], mask, tsem.at[2]), start(accepted_in, accepted, tsem.at[3])]
    own_q = [start(q.at[:, cols(c)], qa[c].at[me], osem_q.at[c]) for c in range(C)]
    own_kv = [start(kv.at[i], kva[i].at[inner], okvsem.at[i]) for i in range(2)]
    pl.semaphore_wait(barrier, n_req + group + n_tp - 3)

    for i in range(2):
        for d in range(1, group):
            send(kv.at[i], kva[i].at[inner], xsem.at[i, d - 1], arsem.at[i, inner], {"seq": other(d)})
    for c in range(C):
        for d in range(n_req - 1, 0, -1):
            send(q.at[:, cols(c)], qa[c].at[me], qsem.at[c, d - 1], qrsem.at[c, me], {"seq": across(d)})
        for d in range(1, group):
            send(q.at[:, cols(c)], qa[c].at[me], qsem.at[c, n_req - 2 + d], qrsem.at[c, me], {"seq": other(d)})

    n_load = min(LOADS, n_slots)
    per = n_slots // n_load
    pool_loads = []
    for i in range(n_load):
        at = pl.ds(i * per, per)
        pool_loads.append(start(pool.at[0, at], kbuf.at[at], ksem.at[i]))
        pool_loads.append(start(pool.at[1, at], vbuf.at[at], vsem.at[i]))
    w_loads = [start(weight.at[:, pl.ds(t * out_w, out_w)], wbuf.at[t], wsem.at[t]) for t in range(n_tp)]

    acc_st[0] = jnp.zeros(acc_st.shape[1:], F32)
    tile[...] = jnp.zeros(tile.shape, F32)
    msg[...] = jnp.zeros(msg.shape, F32)
    writes = []
    for c in tables:
        c.wait()
    shape = table.shape
    index = (lax.broadcasted_iota(jnp.int32, shape, 0) * n_pages + lax.broadcasted_iota(jnp.int32, shape, 1) + 1)
    slots = table[...]
    for r in range(n_req):
        last[r] = 0
    for s in range(n_slots):
        number = jnp.sum(jnp.where(slots == me * n_slots + s, index, 0))
        place = jnp.maximum(number - 1, 0)
        r = jnp.minimum(lax.div(place, n_pages), n_req - 1)
        n = jnp.where(number > 0, cache_len[r] - (place - r * n_pages) * page_len, 0)
        req[s] = r
        left[s] = n
        prev[s] = last[r]
        for i in range(n_req):
            last[i] = jnp.where((n > 0) & (r == i), s + 1, last[i])

    def q_arrived(c, b):
        remote(qa[c].at[b], qa[c].at[b], qsem.at[c, 0], qrsem.at[c, b], {"seq": other(1)}).wait_recv()

    def page_rows(i, r, j):
        return acc_kv.at[i, r, pl.ds(pl.multiple_of(j * rows, rows), rows)]

    def accept():
        for i in range(2):
            own_kv[i].wait()
            for d in range(1, group):
                j = lax.rem(inner + d, group)
                remote(kva[i].at[j], kva[i].at[j], xsem.at[i, 0], arsem.at[i, j], {"seq": other(d)}).wait_recv()
        pick = (lax.broadcasted_iota(jnp.int32, (n_draft, n_draft), 0) == accepted[pl.ds(grp, 1), :]).astype(BF16)
        for i in range(2):
            blocks = jnp.concatenate([kva[i][g] for g in range(group)], axis=0)
            page[i] = lax.dot_general(pick, blocks, TN, preferred_element_type=F32).astype(BF16)
            writes.append(start(page.at[i], acc_kv.at[i, grp], osem.at[i]))
            mine = page.at[i, pl.ds(pl.multiple_of(inner * rows, rows), rows)]
            for side in range(2):
                ahead, to = onward(side)
                send_if(ahead, mine, page_rows(i, grp, inner), asem.at[i, side, 0], krsem.at[i, side, 0, 0], to)

    def onward(side):
        if side == 0:
            return grp + 1 < n_req, {"seq": jnp.minimum(grp + 1, n_req - 1) * group + inner}
        return grp > 0, {"seq": jnp.maximum(grp - 1, 0) * group + inner}

    def source(side, k):
        if side == 0:
            return grp >= k, jnp.maximum(grp - k, 0)
        return grp + k < n_req, jnp.minimum(grp + k, n_req - 1)

    def page_arrived(i, k, e):
        for side in range(2):
            there, r = source(side, k)
            at = page_rows(i, r, lax.rem(inner + group - e, group))
            c = remote(at, at, asem.at[i, 0, 0], krsem.at[i, side, k - 1, e], {"seq": other(1)})
            pl.when(there)(lambda c=c: c.wait_recv())

    def page_onward(i, k):
        page_arrived(i, k, 0)
        if k < n_req - 1:
            for side in range(2):
                there, r = source(side, k)
                ahead, to = onward(side)
                at = page_rows(i, r, inner)
                send_if(there & ahead, at, at, asem.at[i, side, k], krsem.at[i, side, k, 0], to)

    def page_spread(i, k):
        for side in range(2):
            there, r = source(side, k)
            at = page_rows(i, r, inner)
            for e in range(1, group):
                send_if(there, at, at, cfsem.at[i, side, k - 1, e - 1], krsem.at[i, side, k - 1, e], {"seq": other(e)})

    def q_forward(c):
        for e in range(1, n_req):
            b = across(e)
            q_arrived(c, b)
            for d in range(1, group):
                send(qa[c].at[b], qa[c].at[b], fsem.at[c, e - 1, d - 1], qrsem.at[c, b], {"seq": other(d)})

    def q_wait(c):
        for d in range(1, group):
            q_arrived(c, other(d))
            for e in range(1, n_req):
                q_arrived(c, lax.rem(grp + e, n_req) * group + lax.rem(inner + d, group))

    def tree():
        for c in range(C):
            own_q[c].wait()
        allowed = mask[...] == 1
        for h in range(heads):
            c, at = h // hc, slice(h % hc * HD, (h % hc + 1) * HD)
            full = slice(h * HD, (h + 1) * HD)
            keys = jnp.concatenate([kva[0][g, :, full] for g in range(group)], axis=0)
            values = jnp.concatenate([kva[1][g, :, full] for g in range(group)], axis=0)
            x = lax.dot_general(qa[c][me, :, at], keys, NT, preferred_element_type=F32) * scale
            x = jnp.where(allowed, x, NEGATIVE)
            top = jnp.max(x, axis=1, keepdims=True)
            p = jnp.where(allowed, jnp.exp(x - top), 0.0)
            tree_m[h] = jnp.broadcast_to(top, (rows, HD))
            tree_l[h] = jnp.broadcast_to(jnp.sum(p, axis=1, keepdims=True), (rows, HD))
            tree_a[:, full] = jnp.dot(p.astype(BF16), values, preferred_element_type=F32)

    def attend(c):
        blank = jnp.zeros((n_draft, HD), F32)
        for r in range(n_req):
            for k in range(hc // 2):
                for i in range(2):
                    at = slice((2 * k + i) * HD, (2 * k + i + 1) * HD)
                    query = jnp.concatenate([qa[c][r * group + g, :, at] for g in range(group)], axis=0).astype(F32)
                    both = [query, blank] if i == 0 else [blank, query]
                    wq[r, k, i * HD:(i + 1) * HD] = jnp.concatenate(both, axis=0).T.astype(BF16)

        def score(s, carry):
            r = req[s]
            live = lax.broadcasted_iota(jnp.int32, (page_len, HD), 0) < left[s]
            for k in range(hc // 2):
                full = slice(c * cw + 2 * k * HD, c * cw + (2 * k + 2) * HD)
                x = jnp.dot(kbuf[s, :, full], wq[r, k], preferred_element_type=F32)
                x = jnp.where(live, x * scale, NEGATIVE)
                xs[s, k] = x
                m_row[s, k] = jnp.broadcast_to(jnp.max(x, axis=0, keepdims=True), (8, HD))
            return carry

        lax.fori_loop(0, n_slots, score, 0, unroll=min(UNROLL, n_slots))
        for k in range(hc // 2):
            tops = [jnp.full((8, HD), NEGATIVE, F32)] * n_req
            for s in range(n_slots):
                page = m_row[s, k]
                for r in range(n_req):
                    mine = (req[s] == r) & (left[s] > 0)
                    tops[r] = jnp.where(mine, jnp.maximum(tops[r], page), tops[r])
            for r in range(n_req):
                m_top[r, k] = tops[r]

        def weigh(s, carry):
            r = req[s]
            before = prev[s]
            for k in range(hc // 2):
                p = jnp.exp(xs[s, k] - m_top[r, k, 0:1])
                l_row[s, k] = jnp.broadcast_to(jnp.sum(p, axis=0, keepdims=True), (8, HD))
                p = p.T.astype(BF16)
                for i in range(2):
                    h = 2 * k + i
                    at = slice(h * HD, (h + 1) * HD)
                    full = slice(c * cw + h * HD, c * cw + (h + 1) * HD)
                    o = jnp.dot(p[i * n_draft:(i + 1) * n_draft], vbuf[s, :, full], preferred_element_type=F32)
                    acc_st[s + 1, :, at] = acc_st[before, :, at] + o
            return carry

        lax.fori_loop(0, n_slots, weigh, 0, unroll=min(UNROLL, n_slots))
        for k in range(hc // 2):
            sums = [jnp.zeros((8, HD), F32)] * n_req
            for s in range(n_slots):
                page = l_row[s, k]
                for r in range(n_req):
                    mine = (req[s] == r) & (left[s] > 0)
                    sums[r] = jnp.where(mine, sums[r] + page, sums[r])
            for r in range(n_req):
                l_sum[r, k] = sums[r]
        for d in range(n_req):
            r = lax.rem(grp + d, n_req)
            for k in range(pairs):
                row = d * pairs + k
                own_row[c, row:row + 1] = m_top[r, k, 0:1]
                own_row[c, lines + row:lines + row + 1] = l_sum[r, k, 0:1]

    def lanes(h):
        return pl.ds(pl.multiple_of(h % 2 * n_draft + inner * rows, rows), rows)

    order = list(range(n_req - 1, -1, -1))

    def piece(d, j):
        at = last[lax.rem(grp + d, n_req)]
        mine = pl.ds(pl.multiple_of(j * rows, rows), rows)
        return at, mine

    def pack(c):
        for e in range(1, group):
            send(own_row.at[c], their_row.at[c, e - 1], t1sem.at[c, e - 1], t1rsem.at[c, e - 1], {"seq": other(e)})
        for d in order:
            for e in range(1, group):
                at, theirs = piece(d, lax.rem(inner + e, group))
                snd1[c][d, e - 1] = acc_st[at, theirs].astype(BF16)
                send(snd1[c].at[d, e - 1], rcv1[c].at[d, e - 1], s1sem.at[c, d, e - 1], s1rsem.at[c, d, e - 1],
                     {"seq": other(e)})
        for d in order:
            at, mine = piece(d, inner)
            fin_a[c, d] = acc_st[at, mine]

    def merge(c):
        for e in range(1, group):
            remote(own_row.at[c], their_row.at[c, e - 1], t1sem.at[c, e - 1], t1rsem.at[c, e - 1],
                   {"seq": other(e)}).wait_recv()
        tops = [own_row[c, 0:lines]] + [their_row[c, e - 1, 0:lines] for e in range(1, group)]
        sums = [own_row[c, lines:2 * lines]] + [their_row[c, e - 1, lines:2 * lines] for e in range(1, group)]
        top = functools.reduce(jnp.maximum, tops)
        factors = [jnp.exp(m - top) for m in tops]
        both_row[c, 0:lines] = top
        both_row[c, lines:2 * lines] = sum(f * n for f, n in zip(factors, sums))
        for e, f in enumerate(factors):
            tile[e * lines:(e + 1) * lines] = f
        column[c] = tile[...].T
        for d in order:
            for k in range(pairs):
                row = d * pairs + k
                msg[c, d, k:k + 1] = both_row[c, row:row + 1]
                msg[c, d, pairs + k:pairs + k + 1] = both_row[c, lines + row:lines + row + 1]
            if d > 0:
                send(msg.at[c, d], got.at[c, d - 1], t2sem.at[c, d - 1], t2rsem.at[c, d - 1], {"seq": across(d)})
        for d in order:
            for e in range(1, group):
                remote(snd1[c].at[d, e - 1], rcv1[c].at[d, e - 1], s1sem.at[c, d, e - 1], s1rsem.at[c, d, e - 1],
                       {"seq": other(e)}).wait_recv()
            for h in range(hc):
                part = slice(h * HD, (h + 1) * HD)
                f = column[c, lanes(h)]
                row = d * pairs + h // 2
                num = f[:, row:row + 1] * fin_a[c, d, :, part]
                for e in range(1, group):
                    row = e * lines + d * pairs + h // 2
                    num = num + f[:, row:row + 1] * rcv1[c][d, e - 1, :, part].astype(F32)
                if d > 0:
                    snd2[c][d - 1, :, part] = num.astype(BF16)
                else:
                    fin_a[c, 0, :, part] = num
            if d > 0:
                send(snd2[c].at[d - 1], rcv2[c].at[d - 1], s2sem.at[c, d - 1], s2rsem.at[c, d - 1],
                     {"seq": across(d)})

    def finish(c):
        for d in range(1, n_req):
            remote(msg.at[c, d], got.at[c, d - 1], t2sem.at[c, d - 1], t2rsem.at[c, d - 1],
                   {"seq": across(d)}).wait_recv()
        refs = [msg.at[c, 0]] + [got.at[c, d - 1] for d in range(1, n_req)]
        tops = [ref[0:pairs] for ref in refs]
        top = functools.reduce(jnp.maximum, tops)
        factors = [jnp.exp(m - top) for m in tops]
        tile[0:pairs] = top
        tile[pairs:2 * pairs] = sum(f * ref[pairs:2 * pairs] for f, ref in zip(factors, refs))
        for i, f in enumerate(factors):
            tile[(2 + i) * pairs:(3 + i) * pairs] = f
        column[c] = tile[...].T
        for d in range(1, n_req):
            remote(snd2[c].at[d - 1], rcv2[c].at[d - 1], s2sem.at[c, d - 1], s2rsem.at[c, d - 1],
                   {"seq": across(d)}).wait_recv()
        for h in range(hc):
            part = slice(h * HD, (h + 1) * HD)
            full = slice(c * cw + h * HD, c * cw + (h + 1) * HD)
            f = column[c, lanes(h)]

            def at(i):
                return f[:, i * pairs + h // 2:i * pairs + h // 2 + 1]

            cache = at(2) * fin_a[c, 0, :, part]
            for d in range(1, n_req):
                cache = cache + at(2 + d) * rcv2[c][d - 1, :, part].astype(F32)
            mine = tree_m[c * hc + h]
            best = jnp.maximum(at(0), mine)
            g = jnp.exp(at(0) - best)
            t = jnp.exp(mine - best)
            att[:, full] = ((g * cache + t * tree_a[:, full])
                            / (g * at(1) + t * tree_l[c * hc + h])).astype(BF16)

    accept()
    for c in range(C):
        q_forward(c)
        if c == 0:
            tree()
    for c in pool_loads:
        c.wait()
    for c in range(C):
        q_wait(c)
        if c == 0:
            page_onward(0, 1)
            page_onward(1, 1)
        attend(c)
        pack(c)
    page_spread(0, 1)
    page_spread(1, 1)
    for k in range(2, n_req - 1):
        for i in range(2):
            page_onward(i, k)
            page_spread(i, k)
    for c in range(C):
        merge(c)
    for i in range(2):
        page_onward(i, n_req - 1)
        page_spread(i, n_req - 1)
    for c in w_loads:
        c.wait()
    for c in range(C - 1):
        finish(c)
        for t in range(n_tp):
            term = jnp.dot(att[:, c * cw:(c + 1) * cw], wbuf[t, c * cw:(c + 1) * cw], preferred_element_type=F32)
            proj[t] = term if c == 0 else proj[t] + term
    finish(C - 1)
    tail = slice((C - 1) * cw, C * cw)
    y, core = tp // 2, lax.rem(tp, 2)
    peers = [lax.rem(y + a, n_tp // 2) * 2 + lax.rem(core + b, 2) for a in range(n_tp // 2 - 1, -1, -1) for b in range(2)][:-2]
    peers.append(y * 2 + 1 - core)
    for d, peer in enumerate(peers):
        pbuf[d] = (proj[peer] + jnp.dot(att[:, tail], wbuf[peer, tail], preferred_element_type=F32)).astype(BF16)
        send(pbuf.at[d], prbuf.at[d], psem.at[d], prsem.at[d], {"tp": peer})
    total = proj[tp] + jnp.dot(att[:, tail], wbuf[tp, tail], preferred_element_type=F32)
    for d, peer in enumerate(peers):
        remote(pbuf.at[d], prbuf.at[d], psem.at[d], prsem.at[d], {"tp": peer}).wait_recv()
        total = total + prbuf[d].astype(F32)
    out[...] = total.astype(out.dtype)
    for i in range(2):
        for d in range(1, n_req):
            for e in range(1, group):
                page_arrived(i, d, e)
    for c in writes:
        c.wait()
    for c in sent:
        c.wait_send()
    for condition, c in sent_if:
        pl.when(condition)(lambda c=c: c.wait_send())


def copy_kernel(accepted, layer, out, layer_out, held, held_layer, zeros, isem, osem, zsem):
    halves, n_req, n_draft = accepted.shape[:3]
    parts = [(layer, held_layer, layer_out)]
    for c in range(halves):
        for r in range(n_req):
            parts.append((accepted.at[c, r], held.at[c, r], out.at[c, r, pl.ds(0, n_draft)]))
    loads = [pltpu.make_async_copy(a, b, isem.at[i]) for i, (a, b, _) in enumerate(parts)]
    stores = [pltpu.make_async_copy(b, c, osem.at[i]) for i, (_, b, c) in enumerate(parts)]
    for c in loads:
        c.start()
    zeros[...] = jnp.zeros(zeros.shape, zeros.dtype)
    blank = [pltpu.make_async_copy(zeros, out.at[c, r, pl.ds(n_draft, zeros.shape[0])], zsem.at[c, r])
             for c in range(halves) for r in range(n_req)]
    for c in blank:
        c.start()
    for load, store in zip(loads, stores):
        load.wait()
        store.start()
    for c in stores + blank:
        c.wait()


def body(draft_q, draft_kv, kv_pool, page_table, cache_len, tree_mask, accepted_rows, out_weight):
    n_seq = lax.axis_size("seq")
    n_tp = lax.axis_size("tp")
    rows, width = draft_q.shape
    heads = width // HD
    n_req, n_pages = page_table.shape
    n_draft = tree_mask.shape[1]
    n_slots, page_len = kv_pool.shape[1:3]
    group = n_seq // n_req
    out_w = out_weight.shape[1] // n_tp
    C = CHUNKS
    cw = width // C
    hc = heads // C
    dma = pltpu.SemaphoreType.DMA
    vm = pltpu.VMEM
    smem = pltpu.SMEM

    layer, accepted_block = pl.pallas_call(
        functools.partial(fused_kernel, n_req, n_pages, n_seq, n_tp, group),
        out_shape=(jax.ShapeDtypeStruct((rows, out_w), BF16),
                   jax.ShapeDtypeStruct((2, n_req, n_draft, width), BF16)),
        in_specs=[ANY] * 8,
        out_specs=(VMEM, ANY),
        scratch_shapes=[vm((n_seq, rows, cw), BF16)] * C + [vm((group, rows, width), BF16)] * 2
        + [vm((n_req, group - 1, rows, cw), BF16)] * (2 * C)
        + [vm((n_req - 1, rows, cw), BF16)] * (2 * C)
        + [vm(page_table.shape, jnp.int32), smem((n_req,), jnp.int32), vm((rows, n_draft), jnp.int32),
           vm(accepted_rows.shape, jnp.int32),
           vm((2, n_draft, width), BF16),
           vm((n_slots, page_len, width), BF16), vm((n_slots, page_len, width), BF16),
           vm((n_req, hc // 2, 2 * HD, HD), BF16), vm((n_slots, hc // 2, page_len, HD), F32),
           vm((n_slots, hc // 2, 8, HD), F32), vm((n_slots, hc // 2, 8, HD), F32),
           vm((n_req, hc // 2, 8, HD), F32), vm((n_req, hc // 2, 8, HD), F32), vm((C, HD, HD), F32), vm((HD, HD), F32), vm((C, n_req * hc, HD), F32),
           vm((C, group - 1, n_req * hc, HD), F32), vm((C, n_req * hc, HD), F32),
           vm((C, n_req, 8, HD), F32), vm((C, n_req - 1, 8, HD), F32),
           vm((n_slots + 1, n_draft, cw), F32),
           vm((C, n_req, rows, cw), F32),
           vm((heads, rows, HD), F32), vm((heads, rows, HD), F32), vm((rows, width), F32),
           vm((n_tp, width, out_w), BF16), vm((rows, width), BF16), vm((n_tp, rows, out_w), F32),
           vm((n_tp - 1, rows, out_w), BF16), vm((n_tp - 1, rows, out_w), BF16),
           smem((n_slots,), jnp.int32), smem((n_slots,), jnp.int32), smem((n_slots,), jnp.int32),
           smem((n_req,), jnp.int32),
           dma((4,)), dma((C, n_req + group - 2)), dma((C, n_seq)), dma((C, n_req - 1, group - 1)), dma((C,)),
           dma((2, group - 1)), dma((2, group)), dma((2, 2, n_req - 1)), dma((2, 2, n_req - 1, group)),
           dma((2, 2, n_req - 1, group - 1)), dma((2,)),
           dma((LOADS,)), dma((LOADS,)), dma((n_tp,)),
           dma((C, n_req, group - 1)), dma((C, n_req, group - 1)), dma((C, n_req - 1)), dma((C, n_req - 1)),
           dma((n_tp - 1,)), dma((n_tp - 1,)), dma((2,)),
           dma((C, group - 1)), dma((C, group - 1)), dma((C, n_req - 1)), dma((C, n_req - 1))],
        compiler_params=pltpu.CompilerParams(collective_id=0, has_side_effects=True,
                                             vmem_limit_bytes=58 << 20),
        cost_estimate=pl.CostEstimate(flops=10 ** 10, bytes_accessed=3 * 10 ** 7,
                                      transcendentals=10 ** 6),
    )(page_table, cache_len, tree_mask.reshape(n_seq, rows, n_draft), accepted_rows, draft_q, draft_kv, kv_pool,
      out_weight)

    accepted_kv, layer_out = pl.pallas_call(
        copy_kernel,
        out_shape=(jax.ShapeDtypeStruct((2, n_req, page_len, width), BF16),
                   jax.ShapeDtypeStruct((rows, out_w), BF16)),
        in_specs=[ANY, ANY],
        out_specs=(ANY, ANY),
        scratch_shapes=[vm((2, n_req, n_draft, width), BF16), vm((rows, out_w), BF16),
                        vm((page_len - n_draft, width), BF16),
                        dma((2 * n_req + 1,)), dma((2 * n_req + 1,)), dma((2, n_req))],
        compiler_params=pltpu.CompilerParams(vmem_limit_bytes=58 << 20),
    )(accepted_block, layer)
    return (layer_out, accepted_kv)


def solution(mesh):
    return jax.shard_map(
        body,
        mesh=mesh,
        in_specs=(P("seq", "tp"), P(None, "seq", "tp"), P(None, "seq", None, "tp"),
                  P(), P(), P(), P(), P("tp", None)),
        out_specs=(P("seq", "tp"), P(None, None, None, "tp")),
        check_vma=False,
    )
```

```python
import functools
import math

import jax
import jax.numpy as jnp
from jax import lax
from jax.experimental import pallas as pl
from jax.experimental.pallas import tpu as pltpu
from jax.sharding import PartitionSpec as P

HD = 128
CHUNKS = 2
UNROLL = 8
LOADS = 4
NEGATIVE = -1e30
MESH = pl.DeviceIdType.MESH
ANY = pl.BlockSpec(memory_space=pl.ANY)
VMEM = pl.BlockSpec(memory_space=pltpu.VMEM)
NT = (((1,), (1,)), ((), ()))
NN = (((1,), (0,)), ((), ()))
TN = (((0,), (0,)), ((), ()))
F32 = jnp.float32
BF16 = jnp.bfloat16


def fused_kernel(n_req, n_pages, n_seq, n_tp, group, table_in, len_in, mask_in, accepted_in, q, kv, pool, weight,
                 out, acc_kv, *scratch):
    C = CHUNKS
    qa = scratch[:C]
    kva = scratch[C:C + 2]
    snd1 = scratch[C + 2:2 * C + 2]
    rcv1 = scratch[2 * C + 2:3 * C + 2]
    snd2 = scratch[3 * C + 2:4 * C + 2]
    rcv2 = scratch[4 * C + 2:5 * C + 2]
    (table, cache_len, mask, accepted, page, kbuf, vbuf, wq, xs, m_row, l_row, m_top, l_sum, column, tile, own_row, their_row, both_row, msg, got, acc_st,
     fin_a, tree_m, tree_l, tree_a, wbuf, att, proj, pbuf, prbuf, result,
     req, left, prev, last,
     tsem, qsem, qrsem, fsem, osem_q, xsem, arsem, asem, krsem, cfsem, okvsem,
     ksem, vsem, wsem, s1sem, s1rsem, s2sem, s2rsem, psem, prsem, osem,
     t1sem, t1rsem, t2sem, t2rsem) = scratch[5 * C + 2:]
    me = lax.axis_index("seq")
    tp = lax.axis_index("tp")
    grp = me // group
    inner = lax.rem(me, group)
    n_slots, page_len, width = kbuf.shape
    rows, cw = qa[0].shape[1:]
    n_draft = rows * group
    heads = width // HD
    hc = heads // C
    pairs = hc // 2
    lines = n_req * pairs
    out_w = out.shape[1]
    scale = 1.0 / math.sqrt(HD)

    def across(d):
        return lax.rem(grp + d, n_req) * group + inner

    def other(d):
        return grp * group + lax.rem(inner + d, group)

    def remote(a, b, s, r, where):
        return pltpu.make_async_remote_copy(
            src_ref=a, dst_ref=b, send_sem=s, recv_sem=r, device_id=where, device_id_type=MESH)

    sent = []

    def send(*args):
        c = remote(*args)
        c.start()
        sent.append(c)

    sent_if = []

    def send_if(condition, *args):
        c = remote(*args)
        pl.when(condition)(lambda: c.start())
        sent_if.append((condition, c))

    def start(a, b, s):
        c = pltpu.make_async_copy(a, b, s)
        c.start()
        return c

    def cols(c):
        return pl.ds(c * cw, cw)

    barrier = pltpu.get_barrier_semaphore()
    for d in range(1, n_req):
        pl.semaphore_signal(barrier, inc=1, device_id={"seq": across(d)}, device_id_type=MESH)
    for d in range(1, group):
        pl.semaphore_signal(barrier, inc=1, device_id={"seq": other(d)}, device_id_type=MESH)
    for d in range(1, n_tp):
        pl.semaphore_signal(barrier, inc=1, device_id={"tp": lax.rem(tp + d, n_tp)}, device_id_type=MESH)
    tables = [start(table_in, table, tsem.at[0]), start(len_in, cache_len, tsem.at[1]),
              start(mask_in.at[me], mask, tsem.at[2]), start(accepted_in, accepted, tsem.at[3])]
    own_q = [start(q.at[:, cols(c)], qa[c].at[me], osem_q.at[c]) for c in range(C)]
    own_kv = [start(kv.at[i], kva[i].at[inner], okvsem.at[i]) for i in range(2)]
    pl.semaphore_wait(barrier, n_req + group + n_tp - 3)

    for i in range(2):
        for d in range(1, group):
            send(kv.at[i], kva[i].at[inner], xsem.at[i, d - 1], arsem.at[i, inner], {"seq": other(d)})
    for c in range(C):
        for d in range(n_req - 1, 0, -1):
            send(q.at[:, cols(c)], qa[c].at[me], qsem.at[c, d - 1], qrsem.at[c, me], {"seq": across(d)})
        for d in range(1, group):
            send(q.at[:, cols(c)], qa[c].at[me], qsem.at[c, n_req - 2 + d], qrsem.at[c, me], {"seq": other(d)})

    n_load = min(LOADS, n_slots)
    per = n_slots // n_load
    pool_loads = []
    for i in range(n_load):
        at = pl.ds(i * per, per)
        pool_loads.append(start(pool.at[0, at], kbuf.at[at], ksem.at[i]))
        pool_loads.append(start(pool.at[1, at], vbuf.at[at], vsem.at[i]))
    w_loads = [start(weight.at[:, pl.ds(t * out_w, out_w)], wbuf.at[t], wsem.at[t]) for t in range(n_tp)]

    acc_st[0] = jnp.zeros(acc_st.shape[1:], F32)
    tile[...] = jnp.zeros(tile.shape, F32)
    msg[...] = jnp.zeros(msg.shape, F32)
    writes = []
    for c in tables:
        c.wait()
    shape = table.shape
    index = (lax.broadcasted_iota(jnp.int32, shape, 0) * n_pages + lax.broadcasted_iota(jnp.int32, shape, 1) + 1)
    slots = table[...]
    for r in range(n_req):
        last[r] = 0
    for s in range(n_slots):
        number = jnp.sum(jnp.where(slots == me * n_slots + s, index, 0))
        place = jnp.maximum(number - 1, 0)
        r = jnp.minimum(lax.div(place, n_pages), n_req - 1)
        n = jnp.where(number > 0, cache_len[r] - (place - r * n_pages) * page_len, 0)
        req[s] = r
        left[s] = n
        prev[s] = last[r]
        for i in range(n_req):
            last[i] = jnp.where((n > 0) & (r == i), s + 1, last[i])

    def q_arrived(c, b):
        remote(qa[c].at[b], qa[c].at[b], qsem.at[c, 0], qrsem.at[c, b], {"seq": other(1)}).wait_recv()

    def page_rows(i, r, j):
        return acc_kv.at[i, r, pl.ds(pl.multiple_of(j * rows, rows), rows)]

    def accept():
        for i in range(2):
            own_kv[i].wait()
            for d in range(1, group):
                j = lax.rem(inner + d, group)
                remote(kva[i].at[j], kva[i].at[j], xsem.at[i, 0], arsem.at[i, j], {"seq": other(d)}).wait_recv()
        pick = (lax.broadcasted_iota(jnp.int32, (n_draft, n_draft), 0) == accepted[pl.ds(grp, 1), :]).astype(BF16)
        for i in range(2):
            blocks = jnp.concatenate([kva[i][g] for g in range(group)], axis=0)
            page[i] = lax.dot_general(pick, blocks, TN, preferred_element_type=F32).astype(BF16)
            writes.append(start(page.at[i], acc_kv.at[i, grp], osem.at[i]))
            mine = page.at[i, pl.ds(pl.multiple_of(inner * rows, rows), rows)]
            for side in range(2):
                ahead, to = onward(side)
                send_if(ahead, mine, page_rows(i, grp, inner), asem.at[i, side, 0], krsem.at[i, side, 0, 0], to)

    def onward(side):
        if side == 0:
            return grp + 1 < n_req, {"seq": jnp.minimum(grp + 1, n_req - 1) * group + inner}
        return grp > 0, {"seq": jnp.maximum(grp - 1, 0) * group + inner}

    def source(side, k):
        if side == 0:
            return grp >= k, jnp.maximum(grp - k, 0)
        return grp + k < n_req, jnp.minimum(grp + k, n_req - 1)

    def page_arrived(i, k, e):
        for side in range(2):
            there, r = source(side, k)
            at = page_rows(i, r, lax.rem(inner + group - e, group))
            c = remote(at, at, asem.at[i, 0, 0], krsem.at[i, side, k - 1, e], {"seq": other(1)})
            pl.when(there)(lambda c=c: c.wait_recv())

    def page_onward(i, k):
        page_arrived(i, k, 0)
        if k < n_req - 1:
            for side in range(2):
                there, r = source(side, k)
                ahead, to = onward(side)
                at = page_rows(i, r, inner)
                send_if(there & ahead, at, at, asem.at[i, side, k], krsem.at[i, side, k, 0], to)

    def page_spread(i, k):
        for side in range(2):
            there, r = source(side, k)
            at = page_rows(i, r, inner)
            for e in range(1, group):
                send_if(there, at, at, cfsem.at[i, side, k - 1, e - 1], krsem.at[i, side, k - 1, e], {"seq": other(e)})

    def q_forward(c):
        for e in range(1, n_req):
            b = across(e)
            q_arrived(c, b)
            for d in range(1, group):
                send(qa[c].at[b], qa[c].at[b], fsem.at[c, e - 1, d - 1], qrsem.at[c, b], {"seq": other(d)})

    def q_wait(c):
        for d in range(1, group):
            q_arrived(c, other(d))
            for e in range(1, n_req):
                q_arrived(c, lax.rem(grp + e, n_req) * group + lax.rem(inner + d, group))

    def tree():
        for c in range(C):
            own_q[c].wait()
        allowed = mask[...] == 1
        for h in range(heads):
            c, at = h // hc, slice(h % hc * HD, (h % hc + 1) * HD)
            full = slice(h * HD, (h + 1) * HD)
            keys = jnp.concatenate([kva[0][g, :, full] for g in range(group)], axis=0)
            values = jnp.concatenate([kva[1][g, :, full] for g in range(group)], axis=0)
            x = lax.dot_general(qa[c][me, :, at], keys, NT, preferred_element_type=F32) * scale
            x = jnp.where(allowed, x, NEGATIVE)
            top = jnp.max(x, axis=1, keepdims=True)
            p = jnp.where(allowed, jnp.exp(x - top), 0.0)
            tree_m[h] = jnp.broadcast_to(top, (rows, HD))
            tree_l[h] = jnp.broadcast_to(jnp.sum(p, axis=1, keepdims=True), (rows, HD))
            tree_a[:, full] = jnp.dot(p.astype(BF16), values, preferred_element_type=F32)

    def attend(c):
        blank = jnp.zeros((n_draft, HD), F32)
        for r in range(n_req):
            for k in range(hc // 2):
                for i in range(2):
                    at = slice((2 * k + i) * HD, (2 * k + i + 1) * HD)
                    query = jnp.concatenate([qa[c][r * group + g, :, at] for g in range(group)], axis=0).astype(F32)
                    both = [query, blank] if i == 0 else [blank, query]
                    wq[r, k, i * HD:(i + 1) * HD] = jnp.concatenate(both, axis=0).T.astype(BF16)

        def score(s, carry):
            r = req[s]
            live = lax.broadcasted_iota(jnp.int32, (page_len, HD), 0) < left[s]
            for k in range(hc // 2):
                full = slice(c * cw + 2 * k * HD, c * cw + (2 * k + 2) * HD)
                x = jnp.dot(kbuf[s, :, full], wq[r, k], preferred_element_type=F32)
                x = jnp.where(live, x * scale, NEGATIVE)
                xs[s, k] = x
                m_row[s, k] = jnp.broadcast_to(jnp.max(x, axis=0, keepdims=True), (8, HD))
            return carry

        lax.fori_loop(0, n_slots, score, 0, unroll=min(UNROLL, n_slots))
        for k in range(hc // 2):
            tops = [jnp.full((8, HD), NEGATIVE, F32)] * n_req
            for s in range(n_slots):
                page = m_row[s, k]
                for r in range(n_req):
                    mine = (req[s] == r) & (left[s] > 0)
                    tops[r] = jnp.where(mine, jnp.maximum(tops[r], page), tops[r])
            for r in range(n_req):
                m_top[r, k] = tops[r]

        def weigh(s, carry):
            r = req[s]
            before = prev[s]
            for k in range(hc // 2):
                p = jnp.exp(xs[s, k] - m_top[r, k, 0:1])
                l_row[s, k] = jnp.broadcast_to(jnp.sum(p, axis=0, keepdims=True), (8, HD))
                p = p.T.astype(BF16)
                for i in range(2):
                    h = 2 * k + i
                    at = slice(h * HD, (h + 1) * HD)
                    full = slice(c * cw + h * HD, c * cw + (h + 1) * HD)
                    o = jnp.dot(p[i * n_draft:(i + 1) * n_draft], vbuf[s, :, full], preferred_element_type=F32)
                    acc_st[s + 1, :, at] = acc_st[before, :, at] + o
            return carry

        lax.fori_loop(0, n_slots, weigh, 0, unroll=min(UNROLL, n_slots))
        for k in range(hc // 2):
            sums = [jnp.zeros((8, HD), F32)] * n_req
            for s in range(n_slots):
                page = l_row[s, k]
                for r in range(n_req):
                    mine = (req[s] == r) & (left[s] > 0)
                    sums[r] = jnp.where(mine, sums[r] + page, sums[r])
            for r in range(n_req):
                l_sum[r, k] = sums[r]
        for d in range(n_req):
            r = lax.rem(grp + d, n_req)
            for k in range(pairs):
                row = d * pairs + k
                own_row[c, row:row + 1] = m_top[r, k, 0:1]
                own_row[c, lines + row:lines + row + 1] = l_sum[r, k, 0:1]

    def lanes(h):
        return pl.ds(pl.multiple_of(h % 2 * n_draft + inner * rows, rows), rows)

    order = list(range(n_req - 1, -1, -1))

    def piece(d, j):
        at = last[lax.rem(grp + d, n_req)]
        mine = pl.ds(pl.multiple_of(j * rows, rows), rows)
        return at, mine

    def pack(c):
        for e in range(1, group):
            send(own_row.at[c], their_row.at[c, e - 1], t1sem.at[c, e - 1], t1rsem.at[c, e - 1], {"seq": other(e)})
        for d in order:
            for e in range(1, group):
                at, theirs = piece(d, lax.rem(inner + e, group))
                snd1[c][d, e - 1] = acc_st[at, theirs].astype(BF16)
                send(snd1[c].at[d, e - 1], rcv1[c].at[d, e - 1], s1sem.at[c, d, e - 1], s1rsem.at[c, d, e - 1],
                     {"seq": other(e)})
        for d in order:
            at, mine = piece(d, inner)
            fin_a[c, d] = acc_st[at, mine]

    def merge(c):
        for e in range(1, group):
            remote(own_row.at[c], their_row.at[c, e - 1], t1sem.at[c, e - 1], t1rsem.at[c, e - 1],
                   {"seq": other(e)}).wait_recv()
        tops = [own_row[c, 0:lines]] + [their_row[c, e - 1, 0:lines] for e in range(1, group)]
        sums = [own_row[c, lines:2 * lines]] + [their_row[c, e - 1, lines:2 * lines] for e in range(1, group)]
        top = functools.reduce(jnp.maximum, tops)
        factors = [jnp.exp(m - top) for m in tops]
        both_row[c, 0:lines] = top
        both_row[c, lines:2 * lines] = sum(f * n for f, n in zip(factors, sums))
        for e, f in enumerate(factors):
            tile[e * lines:(e + 1) * lines] = f
        column[c] = tile[...].T
        for d in order:
            for k in range(pairs):
                row = d * pairs + k
                msg[c, d, k:k + 1] = both_row[c, row:row + 1]
                msg[c, d, pairs + k:pairs + k + 1] = both_row[c, lines + row:lines + row + 1]
            if d > 0:
                send(msg.at[c, d], got.at[c, d - 1], t2sem.at[c, d - 1], t2rsem.at[c, d - 1], {"seq": across(d)})
        for d in order:
            for e in range(1, group):
                remote(snd1[c].at[d, e - 1], rcv1[c].at[d, e - 1], s1sem.at[c, d, e - 1], s1rsem.at[c, d, e - 1],
                       {"seq": other(e)}).wait_recv()
            for h in range(hc):
                part = slice(h * HD, (h + 1) * HD)
                f = column[c, lanes(h)]
                row = d * pairs + h // 2
                num = f[:, row:row + 1] * fin_a[c, d, :, part]
                for e in range(1, group):
                    row = e * lines + d * pairs + h // 2
                    num = num + f[:, row:row + 1] * rcv1[c][d, e - 1, :, part].astype(F32)
                if d > 0:
                    snd2[c][d - 1, :, part] = num.astype(BF16)
                else:
                    fin_a[c, 0, :, part] = num
            if d > 0:
                send(snd2[c].at[d - 1], rcv2[c].at[d - 1], s2sem.at[c, d - 1], s2rsem.at[c, d - 1],
                     {"seq": across(d)})

    def finish(c):
        for d in range(1, n_req):
            remote(msg.at[c, d], got.at[c, d - 1], t2sem.at[c, d - 1], t2rsem.at[c, d - 1],
                   {"seq": across(d)}).wait_recv()
        refs = [msg.at[c, 0]] + [got.at[c, d - 1] for d in range(1, n_req)]
        tops = [ref[0:pairs] for ref in refs]
        top = functools.reduce(jnp.maximum, tops)
        factors = [jnp.exp(m - top) for m in tops]
        tile[0:pairs] = top
        tile[pairs:2 * pairs] = sum(f * ref[pairs:2 * pairs] for f, ref in zip(factors, refs))
        for i, f in enumerate(factors):
            tile[(2 + i) * pairs:(3 + i) * pairs] = f
        column[c] = tile[...].T
        for d in range(1, n_req):
            remote(snd2[c].at[d - 1], rcv2[c].at[d - 1], s2sem.at[c, d - 1], s2rsem.at[c, d - 1],
                   {"seq": across(d)}).wait_recv()
        for h in range(hc):
            part = slice(h * HD, (h + 1) * HD)
            full = slice(c * cw + h * HD, c * cw + (h + 1) * HD)
            f = column[c, lanes(h)]

            def at(i):
                return f[:, i * pairs + h // 2:i * pairs + h // 2 + 1]

            cache = at(2) * fin_a[c, 0, :, part]
            for d in range(1, n_req):
                cache = cache + at(2 + d) * rcv2[c][d - 1, :, part].astype(F32)
            mine = tree_m[c * hc + h]
            best = jnp.maximum(at(0), mine)
            g = jnp.exp(at(0) - best)
            t = jnp.exp(mine - best)
            att[:, full] = ((g * cache + t * tree_a[:, full])
                            / (g * at(1) + t * tree_l[c * hc + h])).astype(BF16)

    accept()
    for c in range(C):
        q_forward(c)
        if c == 0:
            tree()
    for c in pool_loads:
        c.wait()
    for c in range(C):
        q_wait(c)
        if c == 0:
            page_onward(0, 1)
            page_onward(1, 1)
        attend(c)
        pack(c)
    page_spread(0, 1)
    page_spread(1, 1)
    for k in range(2, n_req - 1):
        for i in range(2):
            page_onward(i, k)
            page_spread(i, k)
    for c in range(C):
        merge(c)
    for i in range(2):
        page_onward(i, n_req - 1)
        page_spread(i, n_req - 1)
    for c in w_loads:
        c.wait()
    for c in range(C - 1):
        finish(c)
        for t in range(n_tp):
            term = jnp.dot(att[:, c * cw:(c + 1) * cw], wbuf[t, c * cw:(c + 1) * cw], preferred_element_type=F32)
            proj[t] = term if c == 0 else proj[t] + term
    finish(C - 1)
    tail = slice((C - 1) * cw, C * cw)
    y, core = tp // 2, lax.rem(tp, 2)
    peers = [lax.rem(y + a, n_tp // 2) * 2 + lax.rem(core + b, 2) for a in range(n_tp // 2 - 1, -1, -1) for b in range(2)][:-2]
    peers.append(y * 2 + 1 - core)
    for d, peer in enumerate(peers):
        pbuf[d] = (proj[peer] + jnp.dot(att[:, tail], wbuf[peer, tail], preferred_element_type=F32)).astype(BF16)
        send(pbuf.at[d], prbuf.at[d], psem.at[d], prsem.at[d], {"tp": peer})
    total = proj[tp] + jnp.dot(att[:, tail], wbuf[tp, tail], preferred_element_type=F32)
    early = len(sent) - len(peers)
    for c in sent[:early]:
        c.wait_send()
    for d, peer in enumerate(peers):
        remote(pbuf.at[d], prbuf.at[d], psem.at[d], prsem.at[d], {"tp": peer}).wait_recv()
        total = total + prbuf[d].astype(F32)
    result[...] = total.astype(out.dtype)
    writes.append(start(result, out, osem.at[2]))
    for i in range(2):
        for d in range(1, n_req):
            for e in range(1, group):
                page_arrived(i, d, e)
    for c in writes:
        c.wait()
    for c in sent[early:]:
        c.wait_send()
    for condition, c in sent_if:
        pl.when(condition)(lambda c=c: c.wait_send())


def copy_kernel(accepted, layer, out, layer_out, held, held_layer, zeros, isem, osem, zsem):
    halves, n_req, n_draft = accepted.shape[:3]
    parts = [(layer, held_layer, layer_out)]
    for c in range(halves):
        for r in range(n_req):
            parts.append((accepted.at[c, r], held.at[c, r], out.at[c, r, pl.ds(0, n_draft)]))
    loads = [pltpu.make_async_copy(a, b, isem.at[i]) for i, (a, b, _) in enumerate(parts)]
    stores = [pltpu.make_async_copy(b, c, osem.at[i]) for i, (_, b, c) in enumerate(parts)]
    for c in loads:
        c.start()
    zeros[...] = jnp.zeros(zeros.shape, zeros.dtype)
    blank = [pltpu.make_async_copy(zeros, out.at[c, r, pl.ds(n_draft, zeros.shape[0])], zsem.at[c, r])
             for c in range(halves) for r in range(n_req)]
    for c in blank:
        c.start()
    for load, store in zip(loads, stores):
        load.wait()
        store.start()
    for c in stores + blank:
        c.wait()


def body(draft_q, draft_kv, kv_pool, page_table, cache_len, tree_mask, accepted_rows, out_weight):
    n_seq = lax.axis_size("seq")
    n_tp = lax.axis_size("tp")
    rows, width = draft_q.shape
    heads = width // HD
    n_req, n_pages = page_table.shape
    n_draft = tree_mask.shape[1]
    n_slots, page_len = kv_pool.shape[1:3]
    group = n_seq // n_req
    out_w = out_weight.shape[1] // n_tp
    C = CHUNKS
    cw = width // C
    hc = heads // C
    dma = pltpu.SemaphoreType.DMA
    vm = pltpu.VMEM
    smem = pltpu.SMEM

    layer, accepted_block = pl.pallas_call(
        functools.partial(fused_kernel, n_req, n_pages, n_seq, n_tp, group),
        out_shape=(jax.ShapeDtypeStruct((rows, out_w), BF16),
                   jax.ShapeDtypeStruct((2, n_req, n_draft, width), BF16)),
        in_specs=[ANY] * 8,
        out_specs=(ANY, ANY),
        scratch_shapes=[vm((n_seq, rows, cw), BF16)] * C + [vm((group, rows, width), BF16)] * 2
        + [vm((n_req, group - 1, rows, cw), BF16)] * (2 * C)
        + [vm((n_req - 1, rows, cw), BF16)] * (2 * C)
        + [vm(page_table.shape, jnp.int32), smem((n_req,), jnp.int32), vm((rows, n_draft), jnp.int32),
           vm(accepted_rows.shape, jnp.int32),
           vm((2, n_draft, width), BF16),
           vm((n_slots, page_len, width), BF16), vm((n_slots, page_len, width), BF16),
           vm((n_req, hc // 2, 2 * HD, HD), BF16), vm((n_slots, hc // 2, page_len, HD), F32),
           vm((n_slots, hc // 2, 8, HD), F32), vm((n_slots, hc // 2, 8, HD), F32),
           vm((n_req, hc // 2, 8, HD), F32), vm((n_req, hc // 2, 8, HD), F32), vm((C, HD, HD), F32), vm((HD, HD), F32), vm((C, n_req * hc, HD), F32),
           vm((C, group - 1, n_req * hc, HD), F32), vm((C, n_req * hc, HD), F32),
           vm((C, n_req, 8, HD), F32), vm((C, n_req - 1, 8, HD), F32),
           vm((n_slots + 1, n_draft, cw), F32),
           vm((C, n_req, rows, cw), F32),
           vm((heads, rows, HD), F32), vm((heads, rows, HD), F32), vm((rows, width), F32),
           vm((n_tp, width, out_w), BF16), vm((rows, width), BF16), vm((n_tp, rows, out_w), F32),
           vm((n_tp - 1, rows, out_w), BF16), vm((n_tp - 1, rows, out_w), BF16), vm((rows, out_w), BF16),
           smem((n_slots,), jnp.int32), smem((n_slots,), jnp.int32), smem((n_slots,), jnp.int32),
           smem((n_req,), jnp.int32),
           dma((4,)), dma((C, n_req + group - 2)), dma((C, n_seq)), dma((C, n_req - 1, group - 1)), dma((C,)),
           dma((2, group - 1)), dma((2, group)), dma((2, 2, n_req - 1)), dma((2, 2, n_req - 1, group)),
           dma((2, 2, n_req - 1, group - 1)), dma((2,)),
           dma((LOADS,)), dma((LOADS,)), dma((n_tp,)),
           dma((C, n_req, group - 1)), dma((C, n_req, group - 1)), dma((C, n_req - 1)), dma((C, n_req - 1)),
           dma((n_tp - 1,)), dma((n_tp - 1,)), dma((3,)),
           dma((C, group - 1)), dma((C, group - 1)), dma((C, n_req - 1)), dma((C, n_req - 1))],
        compiler_params=pltpu.CompilerParams(collective_id=0, has_side_effects=True,
                                             vmem_limit_bytes=58 << 20),
        cost_estimate=pl.CostEstimate(flops=10 ** 10, bytes_accessed=3 * 10 ** 7,
                                      transcendentals=10 ** 6),
    )(page_table, cache_len, tree_mask.reshape(n_seq, rows, n_draft), accepted_rows, draft_q, draft_kv, kv_pool,
      out_weight)

    accepted_kv, layer_out = pl.pallas_call(
        copy_kernel,
        out_shape=(jax.ShapeDtypeStruct((2, n_req, page_len, width), BF16),
                   jax.ShapeDtypeStruct((rows, out_w), BF16)),
        in_specs=[ANY, ANY],
        out_specs=(ANY, ANY),
        scratch_shapes=[vm((2, n_req, n_draft, width), BF16), vm((rows, out_w), BF16),
                        vm((page_len - n_draft, width), BF16),
                        dma((2 * n_req + 1,)), dma((2 * n_req + 1,)), dma((2, n_req))],
        compiler_params=pltpu.CompilerParams(vmem_limit_bytes=58 << 20),
    )(accepted_block, layer)
    return (layer_out, accepted_kv)


def solution(mesh):
    return jax.shard_map(
        body,
        mesh=mesh,
        in_specs=(P("seq", "tp"), P(None, "seq", "tp"), P(None, "seq", None, "tp"),
                  P(), P(), P(), P(), P("tp", None)),
        out_specs=(P("seq", "tp"), P(None, None, None, "tp")),
        check_vma=False,
    )
```
